32 devices in a mesh: group: 2 (over x), seq: 4 (over y, core), fsdp: 4 (over z).
Axes of the slice: x: 2, y: 2, z: 4, core: 2. Of those that a mesh axis runs over, the one named last changes fastest.
Arguments:
- latents: bfloat16 [8192, 3072], P(('group', 'seq', 'fsdp')), parts along dimension 0, may hold values from -6 to 6
- qkv_weight: bfloat16 [3072, 3, 3072], P('seq', None, 'fsdp'), may hold values from -0.109375 to 0.109375
- out_weight: bfloat16 [3072, 3072], P('fsdp', 'seq'), may hold values from -0.109375 to 0.109375
- mod_weight: bfloat16 [256, 3, 3072], P(None, None, ('seq', 'fsdp')), may hold values from -1 to 1
- q_gain: float32 [128], replicated, may hold values from 0.5 to 12, as said below
- k_gain: float32 [128], replicated, may hold values from 0.5 to 12, as said below
- tile_slot: int32 [8, 16], P('group'), parts along dimension 0, may hold values from 0 to 15, each once within a row
- win_start: int32 [8, 16, 3], P('group'), parts along dimension 0, may hold values from 0 to 2, as said below
- step_index: int32 [2], P('group'), parts along dimension 0, may hold values from 0 to 999
Outputs:
- updated: bfloat16 [8192, 3072], P(('group', 'seq', 'fsdp')), parts along dimension 0
The draws below stay inside these ranges and needn't reach their ends.
There are 2 independent parts, one for each index of `group`. The reference program is written for one: setup_inputs(seed, part) draws one part's arguments, and reference() takes and returns one part's arrays. A program takes and returns all parts, laid end to end along the dimension named above; an argument that names none is the same for every part. Nothing has to cross between parts.
Inputs may be any that keep to these rules, and one draw needn't show every extreme that they name: win_start[t, p] holds the first time slice, tile row and tile column of the window of the tile at spatial position p (row p // 4, column p % 4) of slice t; the window spans 2 slices, 3 rows and 3 columns inside the clip and contains the tile itself. `tile_slot`: each row is an ordering of the 16 spatial tiles. `q_gain`: positive gains. `k_gain`: positive gains.
All inputs are finite; a program needn't handle non-finite values.
Results may differ from the reference program's by a relative error of at most 0.014.
The reference program's roundings to bfloat16 on the way (of `signal`, `normed`, `packed` and `attended`) count: a program that leaves them out, or rounds other values in their place, can miss the bound.
Values may be sent and summed in bfloat16 or wider, within the bound.
A program may use at most 192 MiB of HBM per device.

```python
import math
import jax
import jax.numpy as jnp
from jax import lax

D = 3072
H = 24
HD = 128
FREQ = 256
TILE = 64
GH = 4
GW = 4
NT = 4
BLOCK_TOKENS = 1024
TOKENS = 4096
N_SEQ = 4
N_FSDP = 4


def gain_draw(key, which):
    base = jax.random.uniform(jax.random.fold_in(key, which), (HD,), jnp.float32, math.log(0.6), math.log(2.2))
    gain_vec = jnp.exp(base)
    return gain_vec


def draw_q_gain(key, part):
    return gain_draw(key, 1)


def draw_k_gain(key, part):
    return gain_draw(key, 2)


def draw_win_start(key, part):
    spot_count = GH * GW
    time_ids = jnp.arange(NT, dtype=jnp.int32)[:, None] * jnp.ones((1, spot_count), jnp.int32)
    spot_ids = jnp.arange(spot_count, dtype=jnp.int32)[None, :] * jnp.ones((NT, 1), jnp.int32)
    tile_row = spot_ids // GW
    tile_col = spot_ids % GW
    time_lo = jnp.clip(time_ids - 1, 0, NT - 2)
    time_hi = jnp.clip(time_ids, 0, NT - 2)
    row_lo = jnp.clip(tile_row - 2, 0, GH - 3)
    row_hi = jnp.clip(tile_row, 0, GH - 3)
    col_lo = jnp.clip(tile_col - 2, 0, GW - 3)
    col_hi = jnp.clip(tile_col, 0, GW - 3)
    shape_all = (NT, spot_count)
    first_time = jax.random.randint(jax.random.fold_in(key, 3), shape_all, time_lo, time_hi + 1, jnp.int32)
    first_row = jax.random.randint(jax.random.fold_in(key, 4), shape_all, row_lo, row_hi + 1, jnp.int32)
    first_col = jax.random.randint(jax.random.fold_in(key, 5), shape_all, col_lo, col_hi + 1, jnp.int32)
    return jnp.stack([first_time, first_row, first_col], axis=-1).astype(jnp.int32)


def shard_levels(rng, dims, split, low, high):
    gain = 1.0
    for dim, blocks in split:
        draws = jax.random.uniform(jax.random.fold_in(jax.random.fold_in(rng, 6), dim), (blocks,), jnp.float32, low / len(split), high / len(split))
        gain = gain * jnp.repeat(jnp.exp(draws), dims[dim] // blocks).reshape((-1,) + (1,) * (len(dims) - 1 - dim))
    return gain


def centred(key, dims, scale, most, pieces=(), held_as=jnp.bfloat16):
    factor_of = shard_levels(key, dims, pieces, -0.22, 0.18) if pieces else 1.0
    values = jax.random.normal(key, dims, jnp.float32) * scale * factor_of
    return jnp.minimum(jnp.maximum(values, -most), most).astype(held_as)


def setup_inputs(seed: int = 0, part: int = 0) -> dict:
    key_list = jax.random.split(jax.random.key(seed), 10)
    own_keys = jax.random.split(jax.random.fold_in(key_list[9], part), 10)
    latents = centred(own_keys[0], (TOKENS, D), 1.0, 6.0, ((0, 16),))
    qkv_weight = centred(key_list[1], (D, 3, D), D ** -0.5, 0.109375, ((0, 4), (2, 4)))
    out_weight = centred(key_list[2], (D, D), D ** -0.5, 0.109375, ((0, 4), (1, 4)))
    mod_weight = centred(key_list[3], (FREQ, 3, D), 0.15, 1.0, ((2, 16),))
    q_gain = draw_q_gain(jax.random.fold_in(key_list[9], 71), part)
    k_gain = draw_k_gain(jax.random.fold_in(key_list[9], 71), part)
    tile_slot = jax.vmap(lambda own: jax.random.permutation(own, GH * GW))(jax.random.split(own_keys[6], NT)).reshape((NT, GH * GW)).astype(jnp.int32)
    win_start = draw_win_start(jax.random.fold_in(jax.random.fold_in(key_list[9], part), 71), part)
    step_index = jax.random.randint(own_keys[8], (1,), 0, 1000).astype(jnp.int32)
    return dict(latents=latents, qkv_weight=qkv_weight, out_weight=out_weight, mod_weight=mod_weight, q_gain=q_gain, k_gain=k_gain, tile_slot=tile_slot, win_start=win_start, step_index=step_index)


def time_signal(step_index):
    halfway = FREQ // 2
    freqs_all = jnp.exp(-math.log(10000.0) * jnp.arange(halfway, dtype=jnp.float32) / halfway)
    angles = step_index[0].astype(jnp.float32) * freqs_all
    return jax.nn.silu(jnp.concatenate([jnp.cos(angles), jnp.sin(angles)])).astype(jnp.bfloat16)

def modulate(tokens_in, shift_mod, scale_mod):
    values = tokens_in.astype(jnp.float32)
    centre = lax.optimization_barrier(jnp.mean(values, axis=-1, keepdims=True))
    spread = lax.optimization_barrier(jnp.mean((values - centre) ** 2, axis=-1, keepdims=True))
    normal = (values - centre) * lax.rsqrt(spread + 1e-06)
    return (normal * (1.0 + scale_mod) + shift_mod).astype(jnp.bfloat16)

def rms_scale(values, gain_vec):
    return values * lax.rsqrt(lax.optimization_barrier(jnp.mean(values * values, axis=-1, keepdims=True)) + 1e-06) * gain_vec

def project_rows(normed, weight_flat, q_gain, k_gain):
    mixture = jnp.dot(normed, weight_flat, preferred_element_type=jnp.float32)
    row_count = normed.shape[0]
    mixture = mixture.reshape(row_count, 3, -1, HD)
    queries = rms_scale(mixture[:, 0], q_gain)
    key_vecs = rms_scale(mixture[:, 1], k_gain)
    return jnp.stack([queries, key_vecs, mixture[:, 2]], axis=1).reshape(row_count, -1).astype(jnp.bfloat16)

def slot_masks(tile_slot, win_start, block_idx):
    blocks_total = tile_slot.shape[0]
    spot_count = tile_slot.shape[1]
    ids_query = lax.dynamic_index_in_dim(tile_slot, block_idx, 0, keepdims=False)
    window_row = lax.dynamic_index_in_dim(win_start, block_idx, 0, keepdims=False)
    onehot = ids_query[:, None] == jnp.arange(spot_count, dtype=jnp.int32)[None, :]
    corner = lax.optimization_barrier(jnp.sum(jnp.where(onehot[:, :, None], window_row[None], 0), axis=1)).astype(jnp.int32)
    result = []
    for offset in (-1, 0, 1):
        key_time = block_idx + offset
        ids_key = lax.dynamic_index_in_dim(tile_slot, jnp.clip(key_time, 0, blocks_total - 1), 0, keepdims=False)
        tile_row = ids_key // GW
        tile_col = ids_key % GW
        inside = (corner[:, 0:1] <= key_time) & (key_time <= corner[:, 0:1] + 1)
        inside = inside & (corner[:, 1:2] <= tile_row[None]) & (tile_row[None] <= corner[:, 1:2] + 2)
        inside = inside & (corner[:, 2:3] <= tile_col[None]) & (tile_col[None] <= corner[:, 2:3] + 2)
        result.append(jnp.repeat(jnp.repeat(inside, TILE, axis=0), TILE, axis=1))
    return result

def reference(latents, qkv_weight, out_weight, mod_weight, q_gain, k_gain, tile_slot, win_start, step_index):
    signal = time_signal(step_index)
    modulation = jnp.dot(signal[None], mod_weight.reshape(FREQ, 3 * D), preferred_element_type=jnp.float32).reshape(3, D)
    normed = modulate(latents, modulation[0], modulation[1])
    packed = project_rows(normed, qkv_weight.reshape(D, 3 * D), q_gain, k_gain).reshape(TOKENS, 3, H, HD)
    padding = jnp.zeros((BLOCK_TOKENS, H, HD), jnp.bfloat16)
    queries = packed[:, 0]
    key_vecs = jnp.concatenate([padding, packed[:, 1], padding], axis=0)
    value_vecs = jnp.concatenate([padding, packed[:, 2], padding], axis=0)
    inv_root = 1.0 / math.sqrt(HD)

    def one_block(block_idx):
        first_row = block_idx * BLOCK_TOKENS
        q_block = lax.dynamic_slice_in_dim(queries, first_row, BLOCK_TOKENS, 0).astype(jnp.float32)
        k_block = lax.dynamic_slice_in_dim(key_vecs, first_row, 3 * BLOCK_TOKENS, 0).astype(jnp.float32)
        v_block = lax.dynamic_slice_in_dim(value_vecs, first_row, 3 * BLOCK_TOKENS, 0).astype(jnp.float32)
        visible = jnp.concatenate(slot_masks(tile_slot, win_start, block_idx), axis=1)
        scores = jnp.einsum('qhd,khd->hqk', q_block, k_block, precision=lax.Precision.HIGHEST) * inv_root
        shifted = jnp.where(visible[None], scores, -1e+30)
        row_top = lax.optimization_barrier(jnp.max(shifted, axis=-1, keepdims=True))
        weights = jnp.where(visible[None], jnp.exp(shifted - row_top), 0.0)
        totals = lax.optimization_barrier(jnp.sum(weights, axis=-1))
        weights_low = lax.optimization_barrier(weights.astype(jnp.bfloat16)).astype(jnp.float32)
        mixture = jnp.einsum('hqk,khd->qhd', weights_low, v_block, precision=lax.Precision.HIGHEST)
        mixture = mixture / jnp.transpose(totals)[:, :, None]
        return mixture.astype(jnp.bfloat16).reshape(BLOCK_TOKENS, D)
    attended = lax.map(one_block, jnp.arange(N_SEQ, dtype=jnp.int32)).reshape(TOKENS, D)
    group_width = D // N_FSDP
    projected = jnp.zeros((TOKENS, D), jnp.float32)
    for group_idx in range(N_FSDP):
        lower = group_idx * group_width
        part_sum = jnp.dot(attended[:, lower:lower + group_width], out_weight[lower:lower + group_width], preferred_element_type=jnp.float32)
        rounded = lax.optimization_barrier(part_sum.astype(jnp.bfloat16))
        projected = projected + rounded.astype(jnp.float32)
    return (latents.astype(jnp.float32) + modulation[2] * projected).astype(jnp.bfloat16)
```

```python
import functools
import math

import jax
import jax.numpy as jnp
from jax import lax
from jax.experimental import pallas as pl
from jax.experimental.pallas import tpu as pltpu
from jax.sharding import PartitionSpec as P

HD = 128
FREQ = 256
TILE = 64
GW = 4


def with_halo(block, sides, width):
    for axis, dim in sides:
        count = lax.axis_size(axis)
        forward = [(i, i + 1) for i in range(count - 1)]
        backward = [(target, source) for source, target in forward]
        low = lax.ppermute(
            lax.slice_in_dim(block, block.shape[dim] - width, None, axis=dim), axis, forward
        )
        high = lax.ppermute(lax.slice_in_dim(block, 0, width, axis=dim), axis, backward)
        block = jnp.concatenate([low, block, high], axis=dim)
    return block


def time_signal(step_index):
    halfway = FREQ // 2
    freqs_all = jnp.exp(-math.log(10000.0) * jnp.arange(halfway, dtype=jnp.float32) / halfway)
    angles = step_index[0].astype(jnp.float32) * freqs_all
    return jax.nn.silu(jnp.concatenate([jnp.cos(angles), jnp.sin(angles)])).astype(jnp.bfloat16)


def modulate(tokens_in, shift_mod, scale_mod):
    values = tokens_in.astype(jnp.float32)
    centre = jnp.mean(values, axis=-1, keepdims=True)
    spread = jnp.mean((values - centre) ** 2, axis=-1, keepdims=True)
    normal = (values - centre) * lax.rsqrt(spread + 1e-06)
    return (normal * (1.0 + scale_mod) + shift_mod).astype(jnp.bfloat16)


def rms_scale(values, gain_vec):
    return values * lax.rsqrt(jnp.mean(values * values, axis=-1, keepdims=True) + 1e-06) * gain_vec


def project_rows(normed, weight_flat, q_gain, k_gain):
    mixture = jnp.dot(normed, weight_flat, preferred_element_type=jnp.float32)
    row_count = normed.shape[0]
    mixture = mixture.reshape(row_count, 3, -1, HD)
    queries = rms_scale(mixture[:, 0], q_gain)
    key_vecs = rms_scale(mixture[:, 1], k_gain)
    return (
        jnp.stack([queries, key_vecs, mixture[:, 2]], axis=1)
        .reshape(row_count, -1)
        .astype(jnp.bfloat16)
    )


def slot_masks(tile_slot, win_start, block_idx):
    blocks_total = tile_slot.shape[0]
    spot_count = tile_slot.shape[1]
    ids_query = lax.dynamic_index_in_dim(tile_slot, block_idx, 0, keepdims=False)
    window_row = lax.dynamic_index_in_dim(win_start, block_idx, 0, keepdims=False)
    onehot = ids_query[:, None] == jnp.arange(spot_count, dtype=jnp.int32)[None, :]
    corner = jnp.sum(jnp.where(onehot[:, :, None], window_row[None], 0), axis=1)
    result = []
    for offset in (-1, 0, 1):
        key_time = block_idx + offset
        ids_key = lax.dynamic_index_in_dim(
            tile_slot, jnp.clip(key_time, 0, blocks_total - 1), 0, keepdims=False
        )
        tile_row = ids_key // GW
        tile_col = ids_key % GW
        inside = (corner[:, 0:1] <= key_time) & (key_time <= corner[:, 0:1] + 1)
        inside = (
            inside & (corner[:, 1:2] <= tile_row[None]) & (tile_row[None] <= corner[:, 1:2] + 2)
        )
        inside = (
            inside & (corner[:, 2:3] <= tile_col[None]) & (tile_col[None] <= corner[:, 2:3] + 2)
        )
        result.append(jnp.repeat(jnp.repeat(inside, TILE, axis=0), TILE, axis=1))
    return result


def body(
    latents, qkv_weight, out_weight, mod_weight, q_gain, k_gain, tile_slot, win_start, step_index
):
    signal = time_signal(step_index)
    local_cols = mod_weight.shape[2]
    own_mod = jnp.dot(
        signal[None], mod_weight.reshape(FREQ, 3 * local_cols), preferred_element_type=jnp.float32
    ).reshape(3, local_cols)
    modulation = lax.all_gather(own_mod, ("seq", "fsdp"), axis=1, tiled=True)
    shift_mod = modulation[0]
    scale_mod = modulation[1]
    gate_mod = modulation[2]
    qkv_full = lax.all_gather(qkv_weight, "seq", axis=0, tiled=True)
    out_full = lax.all_gather(out_weight, "seq", axis=1, tiled=True)
    model_width = qkv_full.shape[0]
    group_width = qkv_full.shape[2]
    head_count = group_width // HD
    weight_flat = qkv_full.reshape(model_width, 3 * group_width)
    packed = project_rows(
        modulate(lax.all_gather(latents, "fsdp", axis=0, tiled=True), shift_mod, scale_mod),
        weight_flat,
        q_gain,
        k_gain,
    )
    block_tokens = packed.shape[0]
    query_all = packed[:, :group_width].reshape(block_tokens, head_count, HD)
    kv_local = packed[:, group_width:]
    extended = with_halo(kv_local[None], (("seq", 0),), 1)
    key_all = extended[:, :, :group_width].reshape(3, block_tokens, head_count, HD)
    value_all = extended[:, :, group_width:].reshape(3, block_tokens, head_count, HD)
    visible = slot_masks(tile_slot, win_start, lax.axis_index("seq"))
    inv_root = 1.0 / math.sqrt(HD)
    query_span = 512
    head_outputs = []
    for head_idx in range(head_count):
        row_parts = []
        for query_blk in range(block_tokens // query_span):
            lower = query_blk * query_span
            queries = query_all[lower : lower + query_span, head_idx]
            running_top = jnp.full((query_span,), -1e30, jnp.float32)
            running_total = jnp.zeros((query_span,), jnp.float32)
            accum = jnp.zeros((query_span, HD), jnp.float32)
            for key_blk in range(3):
                scores = (
                    lax.dot_general(
                        queries,
                        key_all[key_blk, :, head_idx],
                        (((1,), (1,)), ((), ())),
                        preferred_element_type=jnp.float32,
                    )
                    * inv_root
                )
                allowed = visible[key_blk][lower : lower + query_span]
                shifted = jnp.where(allowed, scores, -1e30)
                new_top = jnp.maximum(running_top, jnp.max(shifted, axis=1))
                weights = jnp.where(allowed, jnp.exp(shifted - new_top[:, None]), 0.0)
                factor = jnp.exp(running_top - new_top)
                running_total = running_total * factor + jnp.sum(weights, axis=1)
                accum = accum * factor[:, None] + jnp.dot(
                    weights.astype(jnp.bfloat16),
                    value_all[key_blk, :, head_idx],
                    preferred_element_type=jnp.float32,
                )
                running_top = new_top
            row_parts.append(accum / running_total[:, None])
        head_outputs.append(jnp.concatenate(row_parts, axis=0))
    attended = (
        jnp.stack(head_outputs, axis=1).reshape(block_tokens, group_width).astype(jnp.bfloat16)
    )
    projected = lax.psum_scatter(
        jnp.dot(attended, out_full, preferred_element_type=jnp.float32).astype(jnp.bfloat16),
        "fsdp",
        scatter_dimension=0,
        tiled=True,
    ).astype(jnp.float32)
    return (latents.astype(jnp.float32) + gate_mod * projected).astype(jnp.bfloat16)

MESH = pl.DeviceIdType.MESH
BF = jnp.bfloat16
F32 = jnp.float32
VMEM_LIMIT = 62 * 1024 * 1024


def entry_barrier(peers):
    barrier = pltpu.get_barrier_semaphore()
    for peer in peers:
        pl.semaphore_signal(barrier, inc=1, device_id=peer, device_id_type=MESH)
    pl.semaphore_wait(barrier, len(peers))


def gather_kernel(
    lat_ref, w_ref, ow_ref, mod_ref, qg_ref, kg_ref,
    q_out, kv_out, ow_all, mod_out,
    lat_all, w_all, mod_all, nrm,
    loc_sem, mod_s, mod_r, lat_s, lat_r, w_s, w_r, ow_s, ow_r, kv_s, kv_r,
):
    s = lax.axis_index("seq")
    z = lax.axis_index("fsdp")
    me = s * 4 + z
    rows = lat_ref.shape[0]
    yp = lax.rem(s + 2, 4)
    cp = s + 1 - 2 * lax.rem(s, 2)
    far = 3 - s

    def flat_peer(step):
        peer = lax.rem(me + step, 16)
        return {"seq": peer // 4, "fsdp": lax.rem(peer, 4)}

    entry_barrier([flat_peer(step) for step in range(1, 16)])

    def remote(src, dst, ss, rs, dev):
        return pltpu.make_async_remote_copy(
            src_ref=src, dst_ref=dst, send_sem=ss, recv_sem=rs, device_id=dev, device_id_type=MESH
        )

    def mod_copy(step):
        return remote(
            mod_ref, mod_all.at[me], mod_s.at[step - 1], mod_r.at[step - 1], flat_peer(step)
        )

    for step in range(1, 16):
        mod_copy(step).start()

    def lat_copy(side, k):
        target = z + 1 if side == 0 else z - 1
        shard = z - k if side == 0 else z + k
        shard = jnp.clip(shard, 0, 3)
        src = lat_ref if k == 0 else lat_all.at[shard]
        return remote(
            src, lat_all.at[shard], lat_s.at[side, k], lat_r.at[side, k], {"fsdp": target}
        )

    def sends(side, k):
        return (z < 3) & (z - k >= 0) if side == 0 else (z > 0) & (z + k <= 3)

    def gets(side, k):
        return z - 1 - k >= 0 if side == 0 else z + 1 + k <= 3

    def start_lat(k):
        for side in range(2):
            @pl.when(sends(side, k))
            def _():
                lat_copy(side, k).start()

    def wait_lat(k):
        for side in range(2):
            @pl.when(gets(side, k))
            def _():
                remote(
                    lat_ref,
                    lat_all.at[jnp.clip(z - 1 - k if side == 0 else z + 1 + k, 0, 3)],
                    lat_s.at[side, k], lat_r.at[side, k], {"fsdp": lax.rem(z + 1, 4)},
                ).wait_recv()

    start_lat(0)

    def w_copy(kind, j):
        if kind == 0:
            return remote(w_ref.at[j], w_all.at[s, j], w_s.at[0, j], w_r.at[0, j], {"seq": yp})
        if kind == 1:
            return remote(w_ref.at[j], w_all.at[s, j], w_s.at[1, j], w_r.at[1, j], {"seq": cp})
        return remote(w_all.at[yp, j], w_all.at[yp, j], w_s.at[2, j], w_r.at[2, j], {"seq": cp})

    def w_wait(kind, j):
        slot = (yp, cp, far)[kind]
        remote(
            w_ref.at[j], w_all.at[slot, j], w_s.at[kind, j], w_r.at[kind, j], {"seq": cp}
        ).wait_recv()

    order = (1, 2, 0)
    for j in order:
        w_copy(0, j).start()
        w_copy(1, j).start()

    local = [
        pltpu.make_async_copy(w_ref, w_all.at[s], loc_sem.at[0]),
        pltpu.make_async_copy(lat_ref, lat_all.at[z], loc_sem.at[1]),
        pltpu.make_async_copy(ow_ref, ow_all.at[s], loc_sem.at[2]),
        pltpu.make_async_copy(mod_ref, mod_all.at[me], loc_sem.at[3]),
    ]
    for copy in local:
        copy.start()

    @pl.when(s == 0)
    def _():
        kv_out[0] = jnp.zeros(kv_out.shape[1:], BF)

    @pl.when(s == 3)
    def _():
        kv_out[2] = jnp.zeros(kv_out.shape[1:], BF)

    for copy in local:
        copy.wait()
    for step in range(1, 16):
        sender = lax.rem(me - step + 16, 16)
        remote(
            mod_ref, mod_all.at[sender], mod_s.at[step - 1], mod_r.at[step - 1], flat_peer(step)
        ).wait_recv()
    mod_out[...] = jnp.concatenate([mod_all[i] for i in range(16)], axis=1)

    w_wait(0, order[0])
    w_copy(2, order[0]).start()
    wait_lat(0)
    start_lat(1)
    w_wait(0, order[1])
    w_copy(2, order[1]).start()
    wait_lat(1)
    start_lat(2)
    w_wait(0, order[2])
    w_copy(2, order[2]).start()

    ow_y = remote(ow_ref, ow_all.at[s], ow_s.at[0], ow_r.at[0], {"seq": yp})
    ow_c = remote(ow_ref, ow_all.at[s], ow_s.at[1], ow_r.at[1], {"seq": cp})
    ow_f = remote(ow_all.at[yp], ow_all.at[yp], ow_s.at[2], ow_r.at[2], {"seq": cp})
    ow_y.start()
    ow_c.start()
    for j in order:
        w_wait(1, j)
        w_wait(2, j)

    def kv_copy(side, i, zz):
        src = kv_out.at[1, pl.ds(pl.multiple_of(zz * rows, rows), rows)]
        dst = kv_out.at[0 if side == 0 else 2, pl.ds(pl.multiple_of(zz * rows, rows), rows)]
        target = s + 1 if side == 0 else s - 1
        return remote(src, dst, kv_s.at[side, i], kv_r.at[side, i], {"seq": target})

    hi = z // 2

    def shard_of(i):
        return lax.rem(i + hi, 4)

    width = w_ref.shape[1]
    lane = 128

    def one_shard(i, carry):
        zz = shard_of(i)

        @pl.when(i == 3)
        def _():
            wait_lat(2)

        def norm_rows(r, c):
            at = pl.ds(pl.multiple_of(r * 32, 32), 32)
            values = lat_all[zz, at, :].astype(F32)
            centre = jnp.mean(values, axis=-1, keepdims=True)
            values = values - centre
            spread = jnp.mean(values * values, axis=-1, keepdims=True)
            normal = values * lax.rsqrt(spread + 1e-06)
            nrm[at, :] = (normal * (1.0 + mod_out[1:2, :]) + mod_out[0:1, :]).astype(BF)
            return c

        lax.fori_loop(0, rows // 32, norm_rows, 0)
        base = pl.ds(pl.multiple_of(zz * rows, rows), rows)
        for j in order:
            for col in range(0, width, 256):
                acc = jnp.zeros((rows, 256), F32)
                for t in range(4):
                    acc = acc + jnp.dot(
                        nrm[:, t * width : (t + 1) * width],
                        w_all[t, j, :, col : col + 256],
                        preferred_element_type=F32,
                    )
                for half in range(0, 256, lane):
                    part = acc[:, half : half + lane]
                    if j < 2:
                        gain = (qg_ref if j == 0 else kg_ref)[...]
                        scale = lax.rsqrt(jnp.mean(part * part, axis=-1, keepdims=True) + 1e-06)
                        part = part * scale * gain
                    part = part.astype(BF)
                    first = col + half
                    if j == 0:
                        q_out[base, first : first + lane] = part
                    else:
                        first = first + (j - 1) * width
                        kv_out[1, base, first : first + lane] = part
            if j == 2:
                @pl.when(s < 3)
                def _():
                    kv_copy(0, i, zz).start()

                @pl.when(s > 0)
                def _():
                    kv_copy(1, i, zz).start()
        return carry

    lax.fori_loop(0, 4, one_shard, 0)

    remote(ow_ref, ow_all.at[yp], ow_s.at[0], ow_r.at[0], {"seq": yp}).wait_recv()
    ow_f.start()
    remote(ow_ref, ow_all.at[cp], ow_s.at[1], ow_r.at[1], {"seq": cp}).wait_recv()
    remote(ow_ref, ow_all.at[far], ow_s.at[2], ow_r.at[2], {"seq": cp}).wait_recv()
    for i in range(4):
        @pl.when(s > 0)
        def _():
            kv_copy(0, i, shard_of(i)).wait_recv()

        @pl.when(s < 3)
        def _():
            kv_copy(1, i, shard_of(i)).wait_recv()
    for i in range(4):
        @pl.when(s < 3)
        def _():
            kv_copy(0, i, shard_of(i)).wait_send()

        @pl.when(s > 0)
        def _():
            kv_copy(1, i, shard_of(i)).wait_send()
    for step in range(1, 16):
        mod_copy(step).wait_send()
    for k in range(3):
        for side in range(2):
            @pl.when(sends(side, k))
            def _():
                lat_copy(side, k).wait_send()
    for kind in range(3):
        for j in range(3):
            w_copy(kind, j).wait_send()
    ow_y.wait_send()
    ow_c.wait_send()
    ow_f.wait_send()


def gather_project(latents, w, ow, mod, q_gain, k_gain):
    rows, model = latents.shape
    width = w.shape[1]
    vmem = pl.BlockSpec(memory_space=pltpu.VMEM)
    dma = pltpu.SemaphoreType.DMA
    return pl.pallas_call(
        gather_kernel,
        out_shape=(
            jax.ShapeDtypeStruct((4 * rows, width), BF),
            jax.ShapeDtypeStruct((3, 4 * rows, 2 * width), BF),
            jax.ShapeDtypeStruct((4,) + ow.shape, BF),
            jax.ShapeDtypeStruct((8, model), F32),
        ),
        in_specs=[vmem] * 6,
        out_specs=(vmem,) * 4,
        scratch_shapes=[
            pltpu.VMEM((4, rows, model), BF),
            pltpu.VMEM((4,) + w.shape, BF),
            pltpu.VMEM((16,) + mod.shape, F32),
            pltpu.VMEM((rows, model), BF),
            dma((4,)), dma((15,)), dma((15,)), dma((2, 3)), dma((2, 3)),
            dma((3, 3)), dma((3, 3)), dma((3,)), dma((3,)), dma((2, 4)), dma((2, 4)),
        ],
        compiler_params=pltpu.CompilerParams(
            collective_id=0, has_side_effects=True, vmem_limit_bytes=VMEM_LIMIT
        ),
    )(latents, w, ow, mod, q_gain, k_gain)


def attend_kernel(q_ref, k_ref, v_ref, bias_ref, o_ref):
    span = q_ref.shape[0]
    keys = k_ref.shape[0] * k_ref.shape[1]
    scores = lax.dot_general(
        q_ref[...], k_ref[...].reshape(keys, HD), (((1,), (1,)), ((), ())),
        preferred_element_type=F32,
    )
    scores = (scores.reshape(span // TILE, TILE, keys) + bias_ref[...]).reshape(span, keys)
    top = jnp.max(scores, axis=1, keepdims=True)
    weights = jnp.exp2((scores - top) * (math.log2(math.e) / math.sqrt(HD)))
    total = jnp.sum(weights, axis=1, keepdims=True)
    mixed = jnp.dot(weights.astype(BF), v_ref[...].reshape(keys, HD), preferred_element_type=F32)
    o_ref[...] = (mixed / total).astype(BF)


def attend(q, kv, bias):
    tokens, width = q.shape
    heads = width // HD
    span = 256
    return pl.pallas_call(
        attend_kernel,
        grid=(heads, tokens // span),
        out_shape=jax.ShapeDtypeStruct((tokens, width), BF),
        in_specs=[
            pl.BlockSpec((span, HD), lambda h, i: (i, h)),
            pl.BlockSpec((3, tokens, HD), lambda h, i: (0, 0, h)),
            pl.BlockSpec((3, tokens, HD), lambda h, i: (0, 0, heads + h)),
            pl.BlockSpec((span // TILE, 1, 3 * tokens), lambda h, i: (i, 0, 0)),
        ],
        out_specs=pl.BlockSpec((span, HD), lambda h, i: (i, h)),
        compiler_params=pltpu.CompilerParams(vmem_limit_bytes=VMEM_LIMIT),
    )(q, kv, kv, bias)


def out_kernel(att_ref, ow_ref, lat_ref, mod_ref, o_ref, sent, got, s_sem, r_sem):
    z = lax.axis_index("fsdp")
    rows = lat_ref.shape[0]
    width = ow_ref.shape[1]
    entry_barrier([{"fsdp": lax.rem(z + step, 4)} for step in range(1, 4)])

    def copy(step):
        return pltpu.make_async_remote_copy(
            src_ref=sent.at[step], dst_ref=got.at[step],
            send_sem=s_sem.at[step], recv_sem=r_sem.at[step],
            device_id={"fsdp": lax.rem(z + step, 4)}, device_id_type=MESH,
        )

    for step in (2, 1, 3, 0):
        goal = lax.rem(z + step, 4)
        base = pl.ds(pl.multiple_of(goal * rows, rows), rows)
        for t in range(4):
            sent[step, :, t * width : (t + 1) * width] = jnp.dot(
                att_ref[base, :], ow_ref[t], preferred_element_type=F32
            ).astype(BF)
        if step:
            copy(step).start()
    for step in range(1, 4):
        copy(step).wait()

    def finish(r, c):
        at = pl.ds(pl.multiple_of(r * 32, 32), 32)
        total = sent[0, at, :].astype(F32)
        for step in range(1, 4):
            total = total + got[step, at, :].astype(F32)
        o_ref[at, :] = (lat_ref[at, :].astype(F32) + mod_ref[2:3, :] * total).astype(BF)
        return c

    lax.fori_loop(0, rows // 32, finish, 0)


def out_project(att, ow_all, latents, mod_full):
    vmem = pl.BlockSpec(memory_space=pltpu.VMEM)
    rows, model = latents.shape
    return pl.pallas_call(
        out_kernel,
        out_shape=jax.ShapeDtypeStruct(latents.shape, BF),
        in_specs=[vmem] * 4,
        out_specs=vmem,
        scratch_shapes=[
            pltpu.VMEM((4, rows, model), BF),
            pltpu.VMEM((4, rows, model), BF),
            pltpu.SemaphoreType.DMA((4,)),
            pltpu.SemaphoreType.DMA((4,)),
        ],
        compiler_params=pltpu.CompilerParams(
            collective_id=1, has_side_effects=True, vmem_limit_bytes=VMEM_LIMIT
        ),
    )(att, ow_all, latents, mod_full)


def key_bias(tile_slot, win_start, block_idx):
    blocks_total, spot_count = tile_slot.shape
    ids_query = lax.dynamic_index_in_dim(tile_slot, block_idx, 0, keepdims=False)
    window_row = lax.dynamic_index_in_dim(win_start, block_idx, 0, keepdims=False)
    onehot = ids_query[:, None] == jnp.arange(spot_count, dtype=jnp.int32)[None, :]
    corner = jnp.sum(jnp.where(onehot[:, :, None], window_row[None], 0), axis=1)
    result = []
    for offset in (-1, 0, 1):
        key_time = block_idx + offset
        ids_key = lax.dynamic_index_in_dim(
            tile_slot, jnp.clip(key_time, 0, blocks_total - 1), 0, keepdims=False
        )
        row = (ids_key // GW)[None]
        col = (ids_key % GW)[None]
        inside = (corner[:, 0:1] <= key_time) & (key_time <= corner[:, 0:1] + 1)
        inside = inside & (corner[:, 1:2] <= row) & (row <= corner[:, 1:2] + 2)
        inside = inside & (corner[:, 2:3] <= col) & (col <= corner[:, 2:3] + 2)
        result.append(inside)
    inside = jnp.concatenate(result, axis=1)
    bias = jnp.where(inside, 0.0, -1e30).astype(F32)
    return jnp.repeat(bias, TILE, axis=1)[:, None, :]


def fast_body(
    latents, qkv_weight, out_weight, mod_weight, q_gain, k_gain, tile_slot, win_start, step_index
):
    signal = time_signal(step_index)
    local_cols = mod_weight.shape[2]
    own_mod = jnp.dot(
        signal[None], mod_weight.reshape(FREQ, 3 * local_cols), preferred_element_type=F32
    ).reshape(3, local_cols)
    own_mod = jnp.pad(own_mod, ((0, 5), (0, 0)))
    w = jnp.transpose(qkv_weight, (1, 0, 2))
    bias = key_bias(tile_slot, win_start, lax.axis_index("seq"))
    q, kv, ow_all, mod_full = gather_project(
        latents, w, out_weight, own_mod, q_gain[None], k_gain[None]
    )
    att = attend(q, kv, bias)
    return out_project(att, ow_all, latents, mod_full)


def solution(mesh):
    in_specs = (
        P(("group", "seq", "fsdp"), None),
        P("seq", None, "fsdp"),
        P("fsdp", "seq"),
        P(None, None, ("seq", "fsdp")),
        P(),
        P(),
        P("group", None),
        P("group", None, None),
        P("group"),
    )
    out_specs = P(("group", "seq", "fsdp"), None)
    small = mesh.shape["seq"] == 4 and mesh.shape["fsdp"] == 4
    return jax.shard_map(
        fast_body if small else body,
        mesh=mesh, in_specs=in_specs, out_specs=out_specs, check_vma=False,
    )
```

```python
import functools
import math

import jax
import jax.numpy as jnp
from jax import lax
from jax.experimental import pallas as pl
from jax.experimental.pallas import tpu as pltpu
from jax.sharding import PartitionSpec as P

HD = 128
FREQ = 256
TILE = 64
GW = 4


def with_halo(block, sides, width):
    for axis, dim in sides:
        count = lax.axis_size(axis)
        forward = [(i, i + 1) for i in range(count - 1)]
        backward = [(target, source) for source, target in forward]
        low = lax.ppermute(
            lax.slice_in_dim(block, block.shape[dim] - width, None, axis=dim), axis, forward
        )
        high = lax.ppermute(lax.slice_in_dim(block, 0, width, axis=dim), axis, backward)
        block = jnp.concatenate([low, block, high], axis=dim)
    return block


def time_signal(step_index):
    halfway = FREQ // 2
    freqs_all = jnp.exp(-math.log(10000.0) * jnp.arange(halfway, dtype=jnp.float32) / halfway)
    angles = step_index[0].astype(jnp.float32) * freqs_all
    return jax.nn.silu(jnp.concatenate([jnp.cos(angles), jnp.sin(angles)])).astype(jnp.bfloat16)


def modulate(tokens_in, shift_mod, scale_mod):
    values = tokens_in.astype(jnp.float32)
    centre = jnp.mean(values, axis=-1, keepdims=True)
    spread = jnp.mean((values - centre) ** 2, axis=-1, keepdims=True)
    normal = (values - centre) * lax.rsqrt(spread + 1e-06)
    return (normal * (1.0 + scale_mod) + shift_mod).astype(jnp.bfloat16)


def rms_scale(values, gain_vec):
    return values * lax.rsqrt(jnp.mean(values * values, axis=-1, keepdims=True) + 1e-06) * gain_vec


def project_rows(normed, weight_flat, q_gain, k_gain):
    mixture = jnp.dot(normed, weight_flat, preferred_element_type=jnp.float32)
    row_count = normed.shape[0]
    mixture = mixture.reshape(row_count, 3, -1, HD)
    queries = rms_scale(mixture[:, 0], q_gain)
    key_vecs = rms_scale(mixture[:, 1], k_gain)
    return (
        jnp.stack([queries, key_vecs, mixture[:, 2]], axis=1)
        .reshape(row_count, -1)
        .astype(jnp.bfloat16)
    )


def slot_masks(tile_slot, win_start, block_idx):
    blocks_total = tile_slot.shape[0]
    spot_count = tile_slot.shape[1]
    ids_query = lax.dynamic_index_in_dim(tile_slot, block_idx, 0, keepdims=False)
    window_row = lax.dynamic_index_in_dim(win_start, block_idx, 0, keepdims=False)
    onehot = ids_query[:, None] == jnp.arange(spot_count, dtype=jnp.int32)[None, :]
    corner = jnp.sum(jnp.where(onehot[:, :, None], window_row[None], 0), axis=1)
    result = []
    for offset in (-1, 0, 1):
        key_time = block_idx + offset
        ids_key = lax.dynamic_index_in_dim(
            tile_slot, jnp.clip(key_time, 0, blocks_total - 1), 0, keepdims=False
        )
        tile_row = ids_key // GW
        tile_col = ids_key % GW
        inside = (corner[:, 0:1] <= key_time) & (key_time <= corner[:, 0:1] + 1)
        inside = (
            inside & (corner[:, 1:2] <= tile_row[None]) & (tile_row[None] <= corner[:, 1:2] + 2)
        )
        inside = (
            inside & (corner[:, 2:3] <= tile_col[None]) & (tile_col[None] <= corner[:, 2:3] + 2)
        )
        result.append(jnp.repeat(jnp.repeat(inside, TILE, axis=0), TILE, axis=1))
    return result


def body(
    latents, qkv_weight, out_weight, mod_weight, q_gain, k_gain, tile_slot, win_start, step_index
):
    signal = time_signal(step_index)
    local_cols = mod_weight.shape[2]
    own_mod = jnp.dot(
        signal[None], mod_weight.reshape(FREQ, 3 * local_cols), preferred_element_type=jnp.float32
    ).reshape(3, local_cols)
    modulation = lax.all_gather(own_mod, ("seq", "fsdp"), axis=1, tiled=True)
    shift_mod = modulation[0]
    scale_mod = modulation[1]
    gate_mod = modulation[2]
    qkv_full = lax.all_gather(qkv_weight, "seq", axis=0, tiled=True)
    out_full = lax.all_gather(out_weight, "seq", axis=1, tiled=True)
    model_width = qkv_full.shape[0]
    group_width = qkv_full.shape[2]
    head_count = group_width // HD
    weight_flat = qkv_full.reshape(model_width, 3 * group_width)
    packed = project_rows(
        modulate(lax.all_gather(latents, "fsdp", axis=0, tiled=True), shift_mod, scale_mod),
        weight_flat,
        q_gain,
        k_gain,
    )
    block_tokens = packed.shape[0]
    query_all = packed[:, :group_width].reshape(block_tokens, head_count, HD)
    kv_local = packed[:, group_width:]
    extended = with_halo(kv_local[None], (("seq", 0),), 1)
    key_all = extended[:, :, :group_width].reshape(3, block_tokens, head_count, HD)
    value_all = extended[:, :, group_width:].reshape(3, block_tokens, head_count, HD)
    visible = slot_masks(tile_slot, win_start, lax.axis_index("seq"))
    inv_root = 1.0 / math.sqrt(HD)
    query_span = 512
    head_outputs = []
    for head_idx in range(head_count):
        row_parts = []
        for query_blk in range(block_tokens // query_span):
            lower = query_blk * query_span
            queries = query_all[lower : lower + query_span, head_idx]
            running_top = jnp.full((query_span,), -1e30, jnp.float32)
            running_total = jnp.zeros((query_span,), jnp.float32)
            accum = jnp.zeros((query_span, HD), jnp.float32)
            for key_blk in range(3):
                scores = (
                    lax.dot_general(
                        queries,
                        key_all[key_blk, :, head_idx],
                        (((1,), (1,)), ((), ())),
                        preferred_element_type=jnp.float32,
                    )
                    * inv_root
                )
                allowed = visible[key_blk][lower : lower + query_span]
                shifted = jnp.where(allowed, scores, -1e30)
                new_top = jnp.maximum(running_top, jnp.max(shifted, axis=1))
                weights = jnp.where(allowed, jnp.exp(shifted - new_top[:, None]), 0.0)
                factor = jnp.exp(running_top - new_top)
                running_total = running_total * factor + jnp.sum(weights, axis=1)
                accum = accum * factor[:, None] + jnp.dot(
                    weights.astype(jnp.bfloat16),
                    value_all[key_blk, :, head_idx],
                    preferred_element_type=jnp.float32,
                )
                running_top = new_top
            row_parts.append(accum / running_total[:, None])
        head_outputs.append(jnp.concatenate(row_parts, axis=0))
    attended = (
        jnp.stack(head_outputs, axis=1).reshape(block_tokens, group_width).astype(jnp.bfloat16)
    )
    projected = lax.psum_scatter(
        jnp.dot(attended, out_full, preferred_element_type=jnp.float32).astype(jnp.bfloat16),
        "fsdp",
        scatter_dimension=0,
        tiled=True,
    ).astype(jnp.float32)
    return (latents.astype(jnp.float32) + gate_mod * projected).astype(jnp.bfloat16)

MESH = pl.DeviceIdType.MESH
BF = jnp.bfloat16
F32 = jnp.float32
VMEM_LIMIT = 62 * 1024 * 1024


def entry_barrier(peers):
    barrier = pltpu.get_barrier_semaphore()
    for peer in peers:
        pl.semaphore_signal(barrier, inc=1, device_id=peer, device_id_type=MESH)
    pl.semaphore_wait(barrier, len(peers))


def gather_kernel(
    lat_ref, w_ref, ow_ref, mod_ref, qg_ref, kg_ref,
    q_out, kv_out, ow_all, mod_out,
    lat_all, w_all, mod_all, nrm,
    loc_sem, mod_s, mod_r, lat_s, lat_r, w_s, w_r, ow_s, ow_r, kv_s, kv_r,
):
    s = lax.axis_index("seq")
    z = lax.axis_index("fsdp")
    me = s * 4 + z
    rows = lat_ref.shape[0]
    yp = lax.rem(s + 2, 4)
    cp = s + 1 - 2 * lax.rem(s, 2)
    far = 3 - s
    g = lax.axis_index("group")
    across = {"group": 1 - g}
    half = w_ref.shape[1] // 2
    mine = pl.ds(pl.multiple_of(g * half, half), half)
    theirs = pl.ds(pl.multiple_of((1 - g) * half, half), half)

    def flat_peer(step):
        peer = lax.rem(me + step, 16)
        return {"seq": peer // 4, "fsdp": lax.rem(peer, 4)}

    entry_barrier([flat_peer(step) for step in range(1, 16)] + [across])

    def remote(src, dst, ss, rs, dev):
        return pltpu.make_async_remote_copy(
            src_ref=src, dst_ref=dst, send_sem=ss, recv_sem=rs, device_id=dev, device_id_type=MESH
        )

    def mod_copy(step):
        return remote(
            mod_ref, mod_all.at[me], mod_s.at[step - 1], mod_r.at[step - 1], flat_peer(step)
        )

    for step in range(1, 16):
        mod_copy(step).start()

    def lat_copy(side, k):
        target = z + 1 if side == 0 else z - 1
        shard = z - k if side == 0 else z + k
        shard = jnp.clip(shard, 0, 3)
        src = lat_ref if k == 0 else lat_all.at[shard]
        return remote(
            src, lat_all.at[shard], lat_s.at[side, k], lat_r.at[side, k], {"fsdp": target}
        )

    def sends(side, k):
        return (z < 3) & (z - k >= 0) if side == 0 else (z > 0) & (z + k <= 3)

    def gets(side, k):
        return z - 1 - k >= 0 if side == 0 else z + 1 + k <= 3

    def start_lat(k):
        for side in range(2):
            @pl.when(sends(side, k))
            def _():
                lat_copy(side, k).start()

    def wait_lat(k):
        for side in range(2):
            @pl.when(gets(side, k))
            def _():
                remote(
                    lat_ref,
                    lat_all.at[jnp.clip(z - 1 - k if side == 0 else z + 1 + k, 0, 3)],
                    lat_s.at[side, k], lat_r.at[side, k], {"fsdp": lax.rem(z + 1, 4)},
                ).wait_recv()

    start_lat(0)

    def spread(own, full, sems_s, sems_r):
        def copy(kind):
            src, dst, dev = (
                (own.at[mine], full.at[s, mine], {"seq": yp}),
                (own, full.at[s], {"seq": cp}),
                (full.at[yp, mine], full.at[yp, mine], {"seq": cp}),
                (full.at[yp, mine], full.at[yp, mine], across),
                (full.at[yp, theirs], full.at[yp, theirs], {"seq": cp}),
            )[kind]
            return remote(src, dst, sems_s.at[kind], sems_r.at[kind], dev)

        def wait(kind):
            slot = (yp, cp, far, yp, far)[kind]
            part = (mine, None, mine, theirs, theirs)[kind]
            src = own if part is None else own.at[part]
            dst = full.at[slot] if part is None else full.at[slot, part]
            remote(src, dst, sems_s.at[kind], sems_r.at[kind], {"seq": cp}).wait_recv()

        return copy, wait

    w_moves = [
        spread(w_ref.at[j], w_all.at[j], w_s.at[j], w_r.at[j]) for j in range(3)
    ]
    ow_copy, ow_wait = spread(ow_ref, ow_all, ow_s, ow_r)

    def w_copy(kind, j):
        return w_moves[j][0](kind)

    def w_wait(kind, j):
        w_moves[j][1](kind)

    def after_y(copy, wait):
        wait(0)
        copy(2).start()
        copy(3).start()

    def after_x(copy, wait):
        wait(3)
        copy(4).start()

    order = (1, 2, 0)
    for j in order:
        w_copy(0, j).start()
        w_copy(1, j).start()

    local = [
        pltpu.make_async_copy(w_ref.at[0], w_all.at[0, s], loc_sem.at[0]),
        pltpu.make_async_copy(w_ref.at[1], w_all.at[1, s], loc_sem.at[4]),
        pltpu.make_async_copy(w_ref.at[2], w_all.at[2, s], loc_sem.at[5]),
        pltpu.make_async_copy(lat_ref, lat_all.at[z], loc_sem.at[1]),
        pltpu.make_async_copy(ow_ref, ow_all.at[s], loc_sem.at[2]),
        pltpu.make_async_copy(mod_ref, mod_all.at[me], loc_sem.at[3]),
    ]
    for copy in local:
        copy.start()

    @pl.when(s == 0)
    def _():
        kv_out[0] = jnp.zeros(kv_out.shape[1:], BF)

    @pl.when(s == 3)
    def _():
        kv_out[2] = jnp.zeros(kv_out.shape[1:], BF)

    for copy in local:
        copy.wait()
    for step in range(1, 16):
        sender = lax.rem(me - step + 16, 16)
        remote(
            mod_ref, mod_all.at[sender], mod_s.at[step - 1], mod_r.at[step - 1], flat_peer(step)
        ).wait_recv()
    mod_out[...] = jnp.concatenate([mod_all[i] for i in range(16)], axis=1)

    after_y(*w_moves[order[0]])
    after_y(*w_moves[order[1]])
    after_x(*w_moves[order[0]])
    wait_lat(0)
    start_lat(1)
    after_y(*w_moves[order[2]])
    ow_copy(0).start()
    ow_copy(1).start()
    after_x(*w_moves[order[1]])
    after_x(*w_moves[order[2]])
    for j in order:
        for kind in (1, 2, 4):
            w_wait(kind, j)

    def kv_copy(side, i, zz):
        src = kv_out.at[1, pl.ds(pl.multiple_of(zz * rows, rows), rows)]
        dst = kv_out.at[0 if side == 0 else 2, pl.ds(pl.multiple_of(zz * rows, rows), rows)]
        target = s + 1 if side == 0 else s - 1
        return remote(src, dst, kv_s.at[side, i], kv_r.at[side, i], {"seq": target})

    hi = z // 2

    def shard_of(i):
        return i + hi * (3 - 2 * i)

    width = w_ref.shape[1]
    lane = 128

    def one_shard(i, carry):
        zz = shard_of(i)

        @pl.when(i == 1)
        def _():
            after_y(ow_copy, ow_wait)

        @pl.when(i == 2)
        def _():
            wait_lat(1)
            start_lat(2)
            after_x(ow_copy, ow_wait)

        @pl.when(i == 3)
        def _():
            wait_lat(2)

        def norm_rows(r, c):
            at = pl.ds(pl.multiple_of(r * 32, 32), 32)
            values = lat_all[zz, at, :].astype(F32)
            centre = jnp.mean(values, axis=-1, keepdims=True)
            values = values - centre
            spread = jnp.mean(values * values, axis=-1, keepdims=True)
            normal = values * lax.rsqrt(spread + 1e-06)
            nrm[at, :] = (normal * (1.0 + mod_out[1:2, :]) + mod_out[0:1, :]).astype(BF)
            return c

        lax.fori_loop(0, rows // 32, norm_rows, 0)
        base = pl.ds(pl.multiple_of(zz * rows, rows), rows)
        for j in order:
            for col in range(0, width, 256):
                acc = jnp.zeros((rows, 256), F32)
                for t in range(4):
                    acc = acc + jnp.dot(
                        nrm[:, t * width : (t + 1) * width],
                        w_all[j, t, :, col : col + 256],
                        preferred_element_type=F32,
                    )
                for half in range(0, 256, lane):
                    part = acc[:, half : half + lane]
                    if j < 2:
                        gain = (qg_ref if j == 0 else kg_ref)[...]
                        scale = lax.rsqrt(jnp.mean(part * part, axis=-1, keepdims=True) + 1e-06)
                        part = part * scale * gain
                    part = part.astype(BF)
                    first = col + half
                    if j == 0:
                        q_out[base, first : first + lane] = part
                    else:
                        first = first + (j - 1) * width
                        kv_out[1, base, first : first + lane] = part
            if j == 2:
                @pl.when(s < 3)
                def _():
                    kv_copy(0, i, zz).start()

                @pl.when(s > 0)
                def _():
                    kv_copy(1, i, zz).start()
        return carry

    lax.fori_loop(0, 4, one_shard, 0)

    for kind in (1, 2, 4):
        ow_wait(kind)
    for i in range(4):
        @pl.when(s > 0)
        def _():
            kv_copy(0, i, shard_of(i)).wait_recv()

        @pl.when(s < 3)
        def _():
            kv_copy(1, i, shard_of(i)).wait_recv()
    for i in range(4):
        @pl.when(s < 3)
        def _():
            kv_copy(0, i, shard_of(i)).wait_send()

        @pl.when(s > 0)
        def _():
            kv_copy(1, i, shard_of(i)).wait_send()
    for step in range(1, 16):
        mod_copy(step).wait_send()
    for k in range(3):
        for side in range(2):
            @pl.when(sends(side, k))
            def _():
                lat_copy(side, k).wait_send()
    for kind in range(5):
        for j in range(3):
            w_copy(kind, j).wait_send()
        ow_copy(kind).wait_send()


def gather_project(latents, w, ow, mod, q_gain, k_gain):
    rows, model = latents.shape
    width = w.shape[1]
    vmem = pl.BlockSpec(memory_space=pltpu.VMEM)
    dma = pltpu.SemaphoreType.DMA
    return pl.pallas_call(
        gather_kernel,
        out_shape=(
            jax.ShapeDtypeStruct((4 * rows, width), BF),
            jax.ShapeDtypeStruct((3, 4 * rows, 2 * width), BF),
            jax.ShapeDtypeStruct((4,) + ow.shape, BF),
            jax.ShapeDtypeStruct((8, model), F32),
        ),
        in_specs=[vmem] * 6,
        out_specs=(vmem,) * 4,
        scratch_shapes=[
            pltpu.VMEM((4, rows, model), BF),
            pltpu.VMEM((3, 4) + w.shape[1:], BF),
            pltpu.VMEM((16,) + mod.shape, F32),
            pltpu.VMEM((rows, model), BF),
            dma((6,)), dma((15,)), dma((15,)), dma((2, 3)), dma((2, 3)),
            dma((3, 5)), dma((3, 5)), dma((5,)), dma((5,)), dma((2, 4)), dma((2, 4)),
        ],
        compiler_params=pltpu.CompilerParams(
            collective_id=0, has_side_effects=True, vmem_limit_bytes=VMEM_LIMIT
        ),
    )(latents, w, ow, mod, q_gain, k_gain)


def attend_out_kernel(
    q_ref, kv_ref, bias_ref, ow_ref, lat_ref, mod_ref, o_ref, att, sent, got, s_sem, r_sem
):
    z = lax.axis_index("fsdp")
    rows = lat_ref.shape[0]
    width = ow_ref.shape[1]
    heads = width // HD
    keys = kv_ref.shape[0] * kv_ref.shape[1]
    hi = z // 2
    far_outer = 3 - 3 * hi
    far_inner = 2 - hi
    near = z + 1 - 2 * lax.rem(z, 2)
    inner = (z == 1) | (z == 2)
    entry_barrier([{"fsdp": lax.rem(z + step, 4)} for step in range(1, 4)])

    def copy(src, dst, goal):
        return pltpu.make_async_remote_copy(
            src_ref=sent.at[src], dst_ref=got.at[dst],
            send_sem=s_sem.at[src], recv_sem=r_sem.at[dst],
            device_id={"fsdp": goal}, device_id_type=MESH,
        )

    to_near = [copy(src, src, near) for src in range(3)]
    to_far = [copy(0, 3, far_outer), copy(1, 3, far_inner)]

    def block(slot, goal):
        base = pl.ds(pl.multiple_of(goal * rows, rows), rows)
        tiles = rows // TILE

        def head(h, c):
            at = pl.ds(pl.multiple_of(h * HD, HD), HD)
            values_at = pl.ds(pl.multiple_of((heads + h) * HD, HD), HD)
            scores = lax.dot_general(
                q_ref[base, at], kv_ref[:, :, at].reshape(keys, HD), (((1,), (1,)), ((), ())),
                preferred_element_type=F32,
            )
            bias = bias_ref[pl.ds(goal * tiles, tiles)]
            scores = (scores.reshape(tiles, TILE, keys) + bias).reshape(rows, keys)
            top = jnp.max(scores, axis=1, keepdims=True)
            weights = jnp.exp2((scores - top) * (math.log2(math.e) / math.sqrt(HD)))
            total = jnp.sum(weights, axis=1, keepdims=True)
            mixed = jnp.dot(
                weights.astype(BF), kv_ref[:, :, values_at].reshape(keys, HD),
                preferred_element_type=F32,
            )
            att[:, at] = (mixed / total).astype(BF)
            return c

        lax.fori_loop(0, heads, head, 0)
        for t in range(4):
            sent[slot, :, t * width : (t + 1) * width] = jnp.dot(
                att[...], ow_ref[t], preferred_element_type=F32
            ).astype(BF)

    def add_near(slot):
        to_near[slot].wait_recv()

        def add(r, c):
            at = pl.ds(pl.multiple_of(r * 32, 32), 32)
            sent[slot, at, :] = (
                sent[slot, at, :].astype(F32) + got[slot, at, :].astype(F32)
            ).astype(BF)
            return c

        lax.fori_loop(0, rows // 32, add, 0)
        to_far[slot].start()

    def step(i, c):
        goal = jnp.where(i == 0, far_outer, jnp.where(i == 1, far_inner, jnp.where(i == 2, near, z)))
        block(i, goal)
        for slot in range(2):
            @pl.when(jnp.logical_not(inner) & (i == slot))
            def _():
                to_near[slot].start()

        @pl.when(i == 2)
        def _():
            to_near[2].start()

        @pl.when(inner & (i == 2))
        def _():
            add_near(0)

        @pl.when(inner & (i == 3))
        def _():
            add_near(1)

        return c

    lax.fori_loop(0, 4, step, 0)
    to_near[2].wait_recv()
    copy(0, 3, far_outer).wait_recv()
    for slot in range(3):
        to_near[slot].wait_send()

    def finish(r, c):
        at = pl.ds(pl.multiple_of(r * 32, 32), 32)
        total = sent[3, at, :].astype(F32)
        total = total + got[2, at, :].astype(F32)
        total = total + got[3, at, :].astype(F32)
        o_ref[at, :] = (lat_ref[at, :].astype(F32) + mod_ref[2:3, :] * total).astype(BF)
        return c

    lax.fori_loop(0, rows // 32, finish, 0)


def attend_out(q, kv, bias, ow_all, latents, mod_full):
    vmem = pl.BlockSpec(memory_space=pltpu.VMEM)
    rows, model = latents.shape
    return pl.pallas_call(
        attend_out_kernel,
        out_shape=jax.ShapeDtypeStruct(latents.shape, BF),
        in_specs=[vmem] * 6,
        out_specs=vmem,
        scratch_shapes=[
            pltpu.VMEM((rows, q.shape[1]), BF),
            pltpu.VMEM((4, rows, model), BF),
            pltpu.VMEM((4, rows, model), BF),
            pltpu.SemaphoreType.DMA((4,)),
            pltpu.SemaphoreType.DMA((4,)),
        ],
        compiler_params=pltpu.CompilerParams(
            collective_id=1, has_side_effects=True, vmem_limit_bytes=VMEM_LIMIT
        ),
    )(q, kv, bias, ow_all, latents, mod_full)


def key_bias(tile_slot, win_start, block_idx):
    blocks_total, spot_count = tile_slot.shape
    ids_query = lax.dynamic_index_in_dim(tile_slot, block_idx, 0, keepdims=False)
    window_row = lax.dynamic_index_in_dim(win_start, block_idx, 0, keepdims=False)
    onehot = ids_query[:, None] == jnp.arange(spot_count, dtype=jnp.int32)[None, :]
    corner = jnp.sum(jnp.where(onehot[:, :, None], window_row[None], 0), axis=1)
    result = []
    for offset in (-1, 0, 1):
        key_time = block_idx + offset
        ids_key = lax.dynamic_index_in_dim(
            tile_slot, jnp.clip(key_time, 0, blocks_total - 1), 0, keepdims=False
        )
        row = (ids_key // GW)[None]
        col = (ids_key % GW)[None]
        inside = (corner[:, 0:1] <= key_time) & (key_time <= corner[:, 0:1] + 1)
        inside = inside & (corner[:, 1:2] <= row) & (row <= corner[:, 1:2] + 2)
        inside = inside & (corner[:, 2:3] <= col) & (col <= corner[:, 2:3] + 2)
        result.append(inside)
    inside = jnp.concatenate(result, axis=1)
    bias = jnp.where(inside, 0.0, -1e30).astype(F32)
    return jnp.repeat(bias, TILE, axis=1)[:, None, :]


def fast_body(
    latents, qkv_weight, out_weight, mod_weight, q_gain, k_gain, tile_slot, win_start, step_index
):
    signal = time_signal(step_index)
    local_cols = mod_weight.shape[2]
    own_mod = jnp.dot(
        signal[None], mod_weight.reshape(FREQ, 3 * local_cols), preferred_element_type=F32
    ).reshape(3, local_cols)
    own_mod = jnp.pad(own_mod, ((0, 5), (0, 0)))
    w = jnp.transpose(qkv_weight, (1, 0, 2))
    bias = key_bias(tile_slot, win_start, lax.axis_index("seq"))
    q, kv, ow_all, mod_full = gather_project(
        latents, w, out_weight, own_mod, q_gain[None], k_gain[None]
    )
    return attend_out(q, kv, bias, ow_all, latents, mod_full)


def solution(mesh):
    in_specs = (
        P(("group", "seq", "fsdp"), None),
        P("seq", None, "fsdp"),
        P("fsdp", "seq"),
        P(None, None, ("seq", "fsdp")),
        P(),
        P(),
        P("group", None),
        P("group", None, None),
        P("group"),
    )
    out_specs = P(("group", "seq", "fsdp"), None)
    small = mesh.shape["seq"] == 4 and mesh.shape["fsdp"] == 4
    return jax.shard_map(
        fast_body if small else body,
        mesh=mesh, in_specs=in_specs, out_specs=out_specs, check_vma=False,
    )
```

```python
import functools
import math

import jax
import jax.numpy as jnp
from jax import lax
from jax.experimental import pallas as pl
from jax.experimental.pallas import tpu as pltpu
from jax.sharding import PartitionSpec as P

HD = 128
FREQ = 256
TILE = 64
GW = 4


def with_halo(block, sides, width):
    for axis, dim in sides:
        count = lax.axis_size(axis)
        forward = [(i, i + 1) for i in range(count - 1)]
        backward = [(target, source) for source, target in forward]
        low = lax.ppermute(
            lax.slice_in_dim(block, block.shape[dim] - width, None, axis=dim), axis, forward
        )
        high = lax.ppermute(lax.slice_in_dim(block, 0, width, axis=dim), axis, backward)
        block = jnp.concatenate([low, block, high], axis=dim)
    return block


def time_signal(step_index):
    halfway = FREQ // 2
    freqs_all = jnp.exp(-math.log(10000.0) * jnp.arange(halfway, dtype=jnp.float32) / halfway)
    angles = step_index[0].astype(jnp.float32) * freqs_all
    return jax.nn.silu(jnp.concatenate([jnp.cos(angles), jnp.sin(angles)])).astype(jnp.bfloat16)


def modulate(tokens_in, shift_mod, scale_mod):
    values = tokens_in.astype(jnp.float32)
    centre = jnp.mean(values, axis=-1, keepdims=True)
    spread = jnp.mean((values - centre) ** 2, axis=-1, keepdims=True)
    normal = (values - centre) * lax.rsqrt(spread + 1e-06)
    return (normal * (1.0 + scale_mod) + shift_mod).astype(jnp.bfloat16)


def rms_scale(values, gain_vec):
    return values * lax.rsqrt(jnp.mean(values * values, axis=-1, keepdims=True) + 1e-06) * gain_vec


def project_rows(normed, weight_flat, q_gain, k_gain):
    mixture = jnp.dot(normed, weight_flat, preferred_element_type=jnp.float32)
    row_count = normed.shape[0]
    mixture = mixture.reshape(row_count, 3, -1, HD)
    queries = rms_scale(mixture[:, 0], q_gain)
    key_vecs = rms_scale(mixture[:, 1], k_gain)
    return (
        jnp.stack([queries, key_vecs, mixture[:, 2]], axis=1)
        .reshape(row_count, -1)
        .astype(jnp.bfloat16)
    )


def slot_masks(tile_slot, win_start, block_idx):
    blocks_total = tile_slot.shape[0]
    spot_count = tile_slot.shape[1]
    ids_query = lax.dynamic_index_in_dim(tile_slot, block_idx, 0, keepdims=False)
    window_row = lax.dynamic_index_in_dim(win_start, block_idx, 0, keepdims=False)
    onehot = ids_query[:, None] == jnp.arange(spot_count, dtype=jnp.int32)[None, :]
    corner = jnp.sum(jnp.where(onehot[:, :, None], window_row[None], 0), axis=1)
    result = []
    for offset in (-1, 0, 1):
        key_time = block_idx + offset
        ids_key = lax.dynamic_index_in_dim(
            tile_slot, jnp.clip(key_time, 0, blocks_total - 1), 0, keepdims=False
        )
        tile_row = ids_key // GW
        tile_col = ids_key % GW
        inside = (corner[:, 0:1] <= key_time) & (key_time <= corner[:, 0:1] + 1)
        inside = (
            inside & (corner[:, 1:2] <= tile_row[None]) & (tile_row[None] <= corner[:, 1:2] + 2)
        )
        inside = (
            inside & (corner[:, 2:3] <= tile_col[None]) & (tile_col[None] <= corner[:, 2:3] + 2)
        )
        result.append(jnp.repeat(jnp.repeat(inside, TILE, axis=0), TILE, axis=1))
    return result


def body(
    latents, qkv_weight, out_weight, mod_weight, q_gain, k_gain, tile_slot, win_start, step_index
):
    signal = time_signal(step_index)
    local_cols = mod_weight.shape[2]
    own_mod = jnp.dot(
        signal[None], mod_weight.reshape(FREQ, 3 * local_cols), preferred_element_type=jnp.float32
    ).reshape(3, local_cols)
    modulation = lax.all_gather(own_mod, ("seq", "fsdp"), axis=1, tiled=True)
    shift_mod = modulation[0]
    scale_mod = modulation[1]
    gate_mod = modulation[2]
    qkv_full = lax.all_gather(qkv_weight, "seq", axis=0, tiled=True)
    out_full = lax.all_gather(out_weight, "seq", axis=1, tiled=True)
    model_width = qkv_full.shape[0]
    group_width = qkv_full.shape[2]
    head_count = group_width // HD
    weight_flat = qkv_full.reshape(model_width, 3 * group_width)
    packed = project_rows(
        modulate(lax.all_gather(latents, "fsdp", axis=0, tiled=True), shift_mod, scale_mod),
        weight_flat,
        q_gain,
        k_gain,
    )
    block_tokens = packed.shape[0]
    query_all = packed[:, :group_width].reshape(block_tokens, head_count, HD)
    kv_local = packed[:, group_width:]
    extended = with_halo(kv_local[None], (("seq", 0),), 1)
    key_all = extended[:, :, :group_width].reshape(3, block_tokens, head_count, HD)
    value_all = extended[:, :, group_width:].reshape(3, block_tokens, head_count, HD)
    visible = slot_masks(tile_slot, win_start, lax.axis_index("seq"))
    inv_root = 1.0 / math.sqrt(HD)
    query_span = 512
    head_outputs = []
    for head_idx in range(head_count):
        row_parts = []
        for query_blk in range(block_tokens // query_span):
            lower = query_blk * query_span
            queries = query_all[lower : lower + query_span, head_idx]
            running_top = jnp.full((query_span,), -1e30, jnp.float32)
            running_total = jnp.zeros((query_span,), jnp.float32)
            accum = jnp.zeros((query_span, HD), jnp.float32)
            for key_blk in range(3):
                scores = (
                    lax.dot_general(
                        queries,
                        key_all[key_blk, :, head_idx],
                        (((1,), (1,)), ((), ())),
                        preferred_element_type=jnp.float32,
                    )
                    * inv_root
                )
                allowed = visible[key_blk][lower : lower + query_span]
                shifted = jnp.where(allowed, scores, -1e30)
                new_top = jnp.maximum(running_top, jnp.max(shifted, axis=1))
                weights = jnp.where(allowed, jnp.exp(shifted - new_top[:, None]), 0.0)
                factor = jnp.exp(running_top - new_top)
                running_total = running_total * factor + jnp.sum(weights, axis=1)
                accum = accum * factor[:, None] + jnp.dot(
                    weights.astype(jnp.bfloat16),
                    value_all[key_blk, :, head_idx],
                    preferred_element_type=jnp.float32,
                )
                running_top = new_top
            row_parts.append(accum / running_total[:, None])
        head_outputs.append(jnp.concatenate(row_parts, axis=0))
    attended = (
        jnp.stack(head_outputs, axis=1).reshape(block_tokens, group_width).astype(jnp.bfloat16)
    )
    projected = lax.psum_scatter(
        jnp.dot(attended, out_full, preferred_element_type=jnp.float32).astype(jnp.bfloat16),
        "fsdp",
        scatter_dimension=0,
        tiled=True,
    ).astype(jnp.float32)
    return (latents.astype(jnp.float32) + gate_mod * projected).astype(jnp.bfloat16)

MESH = pl.DeviceIdType.MESH
BF = jnp.bfloat16
F32 = jnp.float32
VMEM_LIMIT = 62 * 1024 * 1024


def entry_barrier(peers):
    barrier = pltpu.get_barrier_semaphore()
    for peer in peers:
        pl.semaphore_signal(barrier, inc=1, device_id=peer, device_id_type=MESH)
    pl.semaphore_wait(barrier, len(peers))


def gather_kernel(
    lat_ref, w_ref, ow_ref, mod_ref, qg_ref, kg_ref,
    q_out, kv_out, ow_all, mod_out,
    lat_all, w_all, mod_all, nrm,
    loc_sem, mod_s, mod_r, lat_s, lat_r, w_s, w_r, ow_s, ow_r, kv_s, kv_r,
):
    s = lax.axis_index("seq")
    z = lax.axis_index("fsdp")
    me = s * 4 + z
    rows = lat_ref.shape[0]
    yp = lax.rem(s + 2, 4)
    cp = s + 1 - 2 * lax.rem(s, 2)
    far = 3 - s
    g = lax.axis_index("group")
    across = {"group": 1 - g}
    half = w_ref.shape[1] // 2
    mine = pl.ds(pl.multiple_of(g * half, half), half)
    theirs = pl.ds(pl.multiple_of((1 - g) * half, half), half)

    def flat_peer(step):
        peer = lax.rem(me + step, 16)
        return {"seq": peer // 4, "fsdp": lax.rem(peer, 4)}

    entry_barrier([flat_peer(step) for step in range(1, 16)] + [across])

    def remote(src, dst, ss, rs, dev):
        return pltpu.make_async_remote_copy(
            src_ref=src, dst_ref=dst, send_sem=ss, recv_sem=rs, device_id=dev, device_id_type=MESH
        )

    def mod_copy(step):
        return remote(
            mod_ref, mod_all.at[me], mod_s.at[step - 1], mod_r.at[step - 1], flat_peer(step)
        )

    for step in range(1, 16):
        mod_copy(step).start()

    def lat_copy(side, k):
        target = z + 1 if side == 0 else z - 1
        shard = z - k if side == 0 else z + k
        shard = jnp.clip(shard, 0, 3)
        src = lat_ref if k == 0 else lat_all.at[shard]
        return remote(
            src, lat_all.at[shard], lat_s.at[side, k], lat_r.at[side, k], {"fsdp": target}
        )

    def sends(side, k):
        return (z < 3) & (z - k >= 0) if side == 0 else (z > 0) & (z + k <= 3)

    def gets(side, k):
        return z - 1 - k >= 0 if side == 0 else z + 1 + k <= 3

    def start_lat(k):
        for side in range(2):
            @pl.when(sends(side, k))
            def _():
                lat_copy(side, k).start()

    def wait_lat(k):
        for side in range(2):
            @pl.when(gets(side, k))
            def _():
                remote(
                    lat_ref,
                    lat_all.at[jnp.clip(z - 1 - k if side == 0 else z + 1 + k, 0, 3)],
                    lat_s.at[side, k], lat_r.at[side, k], {"fsdp": lax.rem(z + 1, 4)},
                ).wait_recv()

    start_lat(0)

    def spread(own, full, sems_s, sems_r):
        def copy(kind):
            src, dst, dev = (
                (own.at[mine], full.at[s, mine], {"seq": yp}),
                (own, full.at[s], {"seq": cp}),
                (full.at[yp, mine], full.at[yp, mine], {"seq": cp}),
                (full.at[yp, mine], full.at[yp, mine], across),
                (full.at[yp, theirs], full.at[yp, theirs], {"seq": cp}),
            )[kind]
            return remote(src, dst, sems_s.at[kind], sems_r.at[kind], dev)

        def wait(kind):
            slot = (yp, cp, far, yp, far)[kind]
            part = (mine, None, mine, theirs, theirs)[kind]
            src = own if part is None else own.at[part]
            dst = full.at[slot] if part is None else full.at[slot, part]
            remote(src, dst, sems_s.at[kind], sems_r.at[kind], {"seq": cp}).wait_recv()

        return copy, wait

    w_moves = [
        spread(w_ref.at[j], w_all.at[j], w_s.at[j], w_r.at[j]) for j in range(3)
    ]
    ow_copy, ow_wait = spread(ow_ref, ow_all, ow_s, ow_r)

    def w_copy(kind, j):
        return w_moves[j][0](kind)

    def w_wait(kind, j):
        w_moves[j][1](kind)

    def after_y(copy, wait):
        wait(0)
        copy(2).start()
        copy(3).start()

    def after_x(copy, wait):
        wait(3)
        copy(4).start()

    order = (1, 2, 0)
    for j in order:
        w_copy(0, j).start()
        w_copy(1, j).start()

    local = [
        pltpu.make_async_copy(w_ref.at[0], w_all.at[0, s], loc_sem.at[0]),
        pltpu.make_async_copy(w_ref.at[1], w_all.at[1, s], loc_sem.at[4]),
        pltpu.make_async_copy(w_ref.at[2], w_all.at[2, s], loc_sem.at[5]),
        pltpu.make_async_copy(lat_ref, lat_all.at[z], loc_sem.at[1]),
        pltpu.make_async_copy(ow_ref, ow_all.at[s], loc_sem.at[2]),
        pltpu.make_async_copy(mod_ref, mod_all.at[me], loc_sem.at[3]),
    ]
    for copy in local:
        copy.start()

    @pl.when(s == 0)
    def _():
        kv_out[0] = jnp.zeros(kv_out.shape[1:], BF)

    @pl.when(s == 3)
    def _():
        kv_out[2] = jnp.zeros(kv_out.shape[1:], BF)

    for copy in local:
        copy.wait()
    for step in range(1, 16):
        sender = lax.rem(me - step + 16, 16)
        remote(
            mod_ref, mod_all.at[sender], mod_s.at[step - 1], mod_r.at[step - 1], flat_peer(step)
        ).wait_recv()
    mod_out[...] = jnp.concatenate([mod_all[i] for i in range(16)], axis=1)

    after_y(*w_moves[order[0]])
    after_y(*w_moves[order[1]])
    after_x(*w_moves[order[0]])
    wait_lat(0)
    start_lat(1)
    after_y(*w_moves[order[2]])
    ow_copy(0).start()
    ow_copy(1).start()
    after_x(*w_moves[order[1]])
    after_x(*w_moves[order[2]])
    wait_lat(1)
    start_lat(2)
    for j in order:
        for kind in (1, 2, 4):
            w_wait(kind, j)

    def kv_copy(side, i, zz):
        src = kv_out.at[1, pl.ds(pl.multiple_of(zz * rows, rows), rows)]
        dst = kv_out.at[0 if side == 0 else 2, pl.ds(pl.multiple_of(zz * rows, rows), rows)]
        target = s + 1 if side == 0 else s - 1
        return remote(src, dst, kv_s.at[side, i], kv_r.at[side, i], {"seq": target})

    hi = z // 2

    def shard_of(i):
        return i + hi * (3 - 2 * i)

    width = w_ref.shape[1]
    lane = 128

    def one_shard(i, carry):
        zz = shard_of(i)

        @pl.when(i == 1)
        def _():
            after_y(ow_copy, ow_wait)

        @pl.when(i == 2)
        def _():
            after_x(ow_copy, ow_wait)

        @pl.when(i == 3)
        def _():
            wait_lat(2)

        def norm_rows(r, c):
            at = pl.ds(pl.multiple_of(r * 32, 32), 32)
            values = lat_all[zz, at, :].astype(F32)
            centre = jnp.mean(values, axis=-1, keepdims=True)
            values = values - centre
            spread = jnp.mean(values * values, axis=-1, keepdims=True)
            normal = values * lax.rsqrt(spread + 1e-06)
            nrm[at, :] = (normal * (1.0 + mod_out[1:2, :]) + mod_out[0:1, :]).astype(BF)
            return c

        lax.fori_loop(0, rows // 32, norm_rows, 0)
        base = pl.ds(pl.multiple_of(zz * rows, rows), rows)
        for j in order:
            for col in range(0, width, 256):
                acc = jnp.zeros((rows, 256), F32)
                for t in range(4):
                    acc = acc + jnp.dot(
                        nrm[:, t * width : (t + 1) * width],
                        w_all[j, t, :, col : col + 256],
                        preferred_element_type=F32,
                    )
                for half in range(0, 256, lane):
                    part = acc[:, half : half + lane]
                    if j < 2:
                        gain = (qg_ref if j == 0 else kg_ref)[...]
                        scale = lax.rsqrt(jnp.mean(part * part, axis=-1, keepdims=True) + 1e-06)
                        part = part * scale * gain
                    part = part.astype(BF)
                    first = col + half
                    if j == 0:
                        q_out[base, first : first + lane] = part
                    else:
                        first = first + (j - 1) * width
                        kv_out[1, base, first : first + lane] = part
            if j == 2:
                @pl.when(s < 3)
                def _():
                    kv_copy(0, i, zz).start()

                @pl.when(s > 0)
                def _():
                    kv_copy(1, i, zz).start()
        return carry

    lax.fori_loop(0, 4, one_shard, 0)

    for kind in (1, 2, 4):
        ow_wait(kind)
    for i in range(4):
        @pl.when(s > 0)
        def _():
            kv_copy(0, i, shard_of(i)).wait_recv()

        @pl.when(s < 3)
        def _():
            kv_copy(1, i, shard_of(i)).wait_recv()
    for i in range(4):
        @pl.when(s < 3)
        def _():
            kv_copy(0, i, shard_of(i)).wait_send()

        @pl.when(s > 0)
        def _():
            kv_copy(1, i, shard_of(i)).wait_send()
    for step in range(1, 16):
        mod_copy(step).wait_send()
    for k in range(3):
        for side in range(2):
            @pl.when(sends(side, k))
            def _():
                lat_copy(side, k).wait_send()
    for kind in range(5):
        for j in range(3):
            w_copy(kind, j).wait_send()
        ow_copy(kind).wait_send()


def gather_project(latents, w, ow, mod, q_gain, k_gain):
    rows, model = latents.shape
    width = w.shape[1]
    vmem = pl.BlockSpec(memory_space=pltpu.VMEM)
    dma = pltpu.SemaphoreType.DMA
    return pl.pallas_call(
        gather_kernel,
        out_shape=(
            jax.ShapeDtypeStruct((4 * rows, width), BF),
            jax.ShapeDtypeStruct((3, 4 * rows, 2 * width), BF),
            jax.ShapeDtypeStruct((4,) + ow.shape, BF),
            jax.ShapeDtypeStruct((8, model), F32),
        ),
        in_specs=[vmem] * 6,
        out_specs=(vmem,) * 4,
        scratch_shapes=[
            pltpu.VMEM((4, rows, model), BF),
            pltpu.VMEM((3, 4) + w.shape[1:], BF),
            pltpu.VMEM((16,) + mod.shape, F32),
            pltpu.VMEM((rows, model), BF),
            dma((6,)), dma((15,)), dma((15,)), dma((2, 3)), dma((2, 3)),
            dma((3, 5)), dma((3, 5)), dma((5,)), dma((5,)), dma((2, 4)), dma((2, 4)),
        ],
        compiler_params=pltpu.CompilerParams(
            collective_id=0, has_side_effects=True, vmem_limit_bytes=VMEM_LIMIT
        ),
    )(latents, w, ow, mod, q_gain, k_gain)


def attend_out_kernel(
    q_ref, kv_ref, bias_ref, ow_ref, lat_ref, mod_ref, o_ref, att, sent, got, s_sem, r_sem
):
    z = lax.axis_index("fsdp")
    rows = lat_ref.shape[0]
    width = ow_ref.shape[1]
    heads = width // HD
    keys = kv_ref.shape[0] * kv_ref.shape[1]
    hi = z // 2
    far_outer = 3 - 3 * hi
    far_inner = 2 - hi
    near = z + 1 - 2 * lax.rem(z, 2)
    inner = (z == 1) | (z == 2)
    entry_barrier([{"fsdp": lax.rem(z + step, 4)} for step in range(1, 4)])

    def copy(src, dst, goal):
        return pltpu.make_async_remote_copy(
            src_ref=sent.at[src], dst_ref=got.at[dst],
            send_sem=s_sem.at[src], recv_sem=r_sem.at[dst],
            device_id={"fsdp": goal}, device_id_type=MESH,
        )

    to_near = [copy(src, src, near) for src in range(3)]
    to_far = [copy(0, 3, far_outer), copy(1, 3, far_inner)]

    def block(slot, goal):
        base = pl.ds(pl.multiple_of(goal * rows, rows), rows)
        tiles = rows // TILE

        def head(h, c):
            at = pl.ds(pl.multiple_of(h * HD, HD), HD)
            values_at = pl.ds(pl.multiple_of((heads + h) * HD, HD), HD)
            scores = lax.dot_general(
                q_ref[base, at], kv_ref[:, :, at].reshape(keys, HD), (((1,), (1,)), ((), ())),
                preferred_element_type=F32,
            )
            bias = bias_ref[pl.ds(goal * tiles, tiles)]
            scores = (scores.reshape(tiles, TILE, keys) + bias).reshape(rows, keys)
            top = jnp.max(scores, axis=1, keepdims=True)
            weights = jnp.exp2((scores - top) * (math.log2(math.e) / math.sqrt(HD)))
            total = jnp.sum(weights, axis=1, keepdims=True)
            mixed = jnp.dot(
                weights.astype(BF), kv_ref[:, :, values_at].reshape(keys, HD),
                preferred_element_type=F32,
            )
            att[:, at] = (mixed / total).astype(BF)
            return c

        lax.fori_loop(0, heads, head, 0)
        for t in range(4):
            sent[slot, :, t * width : (t + 1) * width] = jnp.dot(
                att[...], ow_ref[t], preferred_element_type=F32
            ).astype(BF)

    def add_near(slot):
        to_near[slot].wait_recv()

        def add(r, c):
            at = pl.ds(pl.multiple_of(r * 32, 32), 32)
            sent[slot, at, :] = (
                sent[slot, at, :].astype(F32) + got[slot, at, :].astype(F32)
            ).astype(BF)
            return c

        lax.fori_loop(0, rows // 32, add, 0)
        to_far[slot].start()

    def step(i, c):
        goal = jnp.where(i == 0, far_outer, jnp.where(i == 1, far_inner, jnp.where(i == 2, near, z)))
        block(i, goal)
        for slot in range(2):
            @pl.when(jnp.logical_not(inner) & (i == slot))
            def _():
                to_near[slot].start()

        @pl.when(i == 2)
        def _():
            to_near[2].start()

        @pl.when(inner & (i == 2))
        def _():
            add_near(0)

        @pl.when(inner & (i == 3))
        def _():
            add_near(1)

        return c

    lax.fori_loop(0, 4, step, 0)
    to_near[2].wait_recv()
    copy(0, 3, far_outer).wait_recv()
    for slot in range(3):
        to_near[slot].wait_send()

    def finish(r, c):
        at = pl.ds(pl.multiple_of(r * 32, 32), 32)
        total = sent[3, at, :].astype(F32)
        total = total + got[2, at, :].astype(F32)
        total = total + got[3, at, :].astype(F32)
        o_ref[at, :] = (lat_ref[at, :].astype(F32) + mod_ref[2:3, :] * total).astype(BF)
        return c

    lax.fori_loop(0, rows // 32, finish, 0)


def attend_out(q, kv, bias, ow_all, latents, mod_full):
    vmem = pl.BlockSpec(memory_space=pltpu.VMEM)
    rows, model = latents.shape
    return pl.pallas_call(
        attend_out_kernel,
        out_shape=jax.ShapeDtypeStruct(latents.shape, BF),
        in_specs=[vmem] * 6,
        out_specs=vmem,
        scratch_shapes=[
            pltpu.VMEM((rows, q.shape[1]), BF),
            pltpu.VMEM((4, rows, model), BF),
            pltpu.VMEM((4, rows, model), BF),
            pltpu.SemaphoreType.DMA((4,)),
            pltpu.SemaphoreType.DMA((4,)),
        ],
        compiler_params=pltpu.CompilerParams(
            collective_id=1, has_side_effects=True, vmem_limit_bytes=VMEM_LIMIT
        ),
    )(q, kv, bias, ow_all, latents, mod_full)


def key_bias(tile_slot, win_start, block_idx):
    blocks_total, spot_count = tile_slot.shape
    ids_query = lax.dynamic_index_in_dim(tile_slot, block_idx, 0, keepdims=False)
    window_row = lax.dynamic_index_in_dim(win_start, block_idx, 0, keepdims=False)
    onehot = ids_query[:, None] == jnp.arange(spot_count, dtype=jnp.int32)[None, :]
    corner = jnp.sum(jnp.where(onehot[:, :, None], window_row[None], 0), axis=1)
    result = []
    for offset in (-1, 0, 1):
        key_time = block_idx + offset
        ids_key = lax.dynamic_index_in_dim(
            tile_slot, jnp.clip(key_time, 0, blocks_total - 1), 0, keepdims=False
        )
        row = (ids_key // GW)[None]
        col = (ids_key % GW)[None]
        inside = (corner[:, 0:1] <= key_time) & (key_time <= corner[:, 0:1] + 1)
        inside = inside & (corner[:, 1:2] <= row) & (row <= corner[:, 1:2] + 2)
        inside = inside & (corner[:, 2:3] <= col) & (col <= corner[:, 2:3] + 2)
        result.append(inside)
    inside = jnp.concatenate(result, axis=1)
    bias = jnp.where(inside, 0.0, -1e30).astype(F32)
    return jnp.repeat(bias, TILE, axis=1)[:, None, :]


def fast_body(
    latents, qkv_weight, out_weight, mod_weight, q_gain, k_gain, tile_slot, win_start, step_index
):
    signal = time_signal(step_index)
    local_cols = mod_weight.shape[2]
    own_mod = jnp.dot(
        signal[None], mod_weight.reshape(FREQ, 3 * local_cols), preferred_element_type=F32
    ).reshape(3, local_cols)
    own_mod = jnp.pad(own_mod, ((0, 5), (0, 0)))
    w = jnp.transpose(qkv_weight, (1, 0, 2))
    bias = key_bias(tile_slot, win_start, lax.axis_index("seq"))
    q, kv, ow_all, mod_full = gather_project(
        latents, w, out_weight, own_mod, q_gain[None], k_gain[None]
    )
    return attend_out(q, kv, bias, ow_all, latents, mod_full)


def solution(mesh):
    in_specs = (
        P(("group", "seq", "fsdp"), None),
        P("seq", None, "fsdp"),
        P("fsdp", "seq"),
        P(None, None, ("seq", "fsdp")),
        P(),
        P(),
        P("group", None),
        P("group", None, None),
        P("group"),
    )
    out_specs = P(("group", "seq", "fsdp"), None)
    small = mesh.shape["seq"] == 4 and mesh.shape["fsdp"] == 4
    return jax.shard_map(
        fast_body if small else body,
        mesh=mesh, in_specs=in_specs, out_specs=out_specs, check_vma=False,
    )
```

```python
import functools
import math

import jax
import jax.numpy as jnp
from jax import lax
from jax.experimental import pallas as pl
from jax.experimental.pallas import tpu as pltpu
from jax.sharding import PartitionSpec as P

HD = 128
FREQ = 256
TILE = 64
GW = 4


def with_halo(block, sides, width):
    for axis, dim in sides:
        count = lax.axis_size(axis)
        forward = [(i, i + 1) for i in range(count - 1)]
        backward = [(target, source) for source, target in forward]
        low = lax.ppermute(
            lax.slice_in_dim(block, block.shape[dim] - width, None, axis=dim), axis, forward
        )
        high = lax.ppermute(lax.slice_in_dim(block, 0, width, axis=dim), axis, backward)
        block = jnp.concatenate([low, block, high], axis=dim)
    return block


def time_signal(step_index):
    halfway = FREQ // 2
    freqs_all = jnp.exp(-math.log(10000.0) * jnp.arange(halfway, dtype=jnp.float32) / halfway)
    angles = step_index[0].astype(jnp.float32) * freqs_all
    return jax.nn.silu(jnp.concatenate([jnp.cos(angles), jnp.sin(angles)])).astype(jnp.bfloat16)


def modulate(tokens_in, shift_mod, scale_mod):
    values = tokens_in.astype(jnp.float32)
    centre = jnp.mean(values, axis=-1, keepdims=True)
    spread = jnp.mean((values - centre) ** 2, axis=-1, keepdims=True)
    normal = (values - centre) * lax.rsqrt(spread + 1e-06)
    return (normal * (1.0 + scale_mod) + shift_mod).astype(jnp.bfloat16)


def rms_scale(values, gain_vec):
    return values * lax.rsqrt(jnp.mean(values * values, axis=-1, keepdims=True) + 1e-06) * gain_vec


def project_rows(normed, weight_flat, q_gain, k_gain):
    mixture = jnp.dot(normed, weight_flat, preferred_element_type=jnp.float32)
    row_count = normed.shape[0]
    mixture = mixture.reshape(row_count, 3, -1, HD)
    queries = rms_scale(mixture[:, 0], q_gain)
    key_vecs = rms_scale(mixture[:, 1], k_gain)
    return (
        jnp.stack([queries, key_vecs, mixture[:, 2]], axis=1)
        .reshape(row_count, -1)
        .astype(jnp.bfloat16)
    )


def slot_masks(tile_slot, win_start, block_idx):
    blocks_total = tile_slot.shape[0]
    spot_count = tile_slot.shape[1]
    ids_query = lax.dynamic_index_in_dim(tile_slot, block_idx, 0, keepdims=False)
    window_row = lax.dynamic_index_in_dim(win_start, block_idx, 0, keepdims=False)
    onehot = ids_query[:, None] == jnp.arange(spot_count, dtype=jnp.int32)[None, :]
    corner = jnp.sum(jnp.where(onehot[:, :, None], window_row[None], 0), axis=1)
    result = []
    for offset in (-1, 0, 1):
        key_time = block_idx + offset
        ids_key = lax.dynamic_index_in_dim(
            tile_slot, jnp.clip(key_time, 0, blocks_total - 1), 0, keepdims=False
        )
        tile_row = ids_key // GW
        tile_col = ids_key % GW
        inside = (corner[:, 0:1] <= key_time) & (key_time <= corner[:, 0:1] + 1)
        inside = (
            inside & (corner[:, 1:2] <= tile_row[None]) & (tile_row[None] <= corner[:, 1:2] + 2)
        )
        inside = (
            inside & (corner[:, 2:3] <= tile_col[None]) & (tile_col[None] <= corner[:, 2:3] + 2)
        )
        result.append(jnp.repeat(jnp.repeat(inside, TILE, axis=0), TILE, axis=1))
    return result


def body(
    latents, qkv_weight, out_weight, mod_weight, q_gain, k_gain, tile_slot, win_start, step_index
):
    signal = time_signal(step_index)
    local_cols = mod_weight.shape[2]
    own_mod = jnp.dot(
        signal[None], mod_weight.reshape(FREQ, 3 * local_cols), preferred_element_type=jnp.float32
    ).reshape(3, local_cols)
    modulation = lax.all_gather(own_mod, ("seq", "fsdp"), axis=1, tiled=True)
    shift_mod = modulation[0]
    scale_mod = modulation[1]
    gate_mod = modulation[2]
    qkv_full = lax.all_gather(qkv_weight, "seq", axis=0, tiled=True)
    out_full = lax.all_gather(out_weight, "seq", axis=1, tiled=True)
    model_width = qkv_full.shape[0]
    group_width = qkv_full.shape[2]
    head_count = group_width // HD
    weight_flat = qkv_full.reshape(model_width, 3 * group_width)
    packed = project_rows(
        modulate(lax.all_gather(latents, "fsdp", axis=0, tiled=True), shift_mod, scale_mod),
        weight_flat,
        q_gain,
        k_gain,
    )
    block_tokens = packed.shape[0]
    query_all = packed[:, :group_width].reshape(block_tokens, head_count, HD)
    kv_local = packed[:, group_width:]
    extended = with_halo(kv_local[None], (("seq", 0),), 1)
    key_all = extended[:, :, :group_width].reshape(3, block_tokens, head_count, HD)
    value_all = extended[:, :, group_width:].reshape(3, block_tokens, head_count, HD)
    visible = slot_masks(tile_slot, win_start, lax.axis_index("seq"))
    inv_root = 1.0 / math.sqrt(HD)
    query_span = 512
    head_outputs = []
    for head_idx in range(head_count):
        row_parts = []
        for query_blk in range(block_tokens // query_span):
            lower = query_blk * query_span
            queries = query_all[lower : lower + query_span, head_idx]
            running_top = jnp.full((query_span,), -1e30, jnp.float32)
            running_total = jnp.zeros((query_span,), jnp.float32)
            accum = jnp.zeros((query_span, HD), jnp.float32)
            for key_blk in range(3):
                scores = (
                    lax.dot_general(
                        queries,
                        key_all[key_blk, :, head_idx],
                        (((1,), (1,)), ((), ())),
                        preferred_element_type=jnp.float32,
                    )
                    * inv_root
                )
                allowed = visible[key_blk][lower : lower + query_span]
                shifted = jnp.where(allowed, scores, -1e30)
                new_top = jnp.maximum(running_top, jnp.max(shifted, axis=1))
                weights = jnp.where(allowed, jnp.exp(shifted - new_top[:, None]), 0.0)
                factor = jnp.exp(running_top - new_top)
                running_total = running_total * factor + jnp.sum(weights, axis=1)
                accum = accum * factor[:, None] + jnp.dot(
                    weights.astype(jnp.bfloat16),
                    value_all[key_blk, :, head_idx],
                    preferred_element_type=jnp.float32,
                )
                running_top = new_top
            row_parts.append(accum / running_total[:, None])
        head_outputs.append(jnp.concatenate(row_parts, axis=0))
    attended = (
        jnp.stack(head_outputs, axis=1).reshape(block_tokens, group_width).astype(jnp.bfloat16)
    )
    projected = lax.psum_scatter(
        jnp.dot(attended, out_full, preferred_element_type=jnp.float32).astype(jnp.bfloat16),
        "fsdp",
        scatter_dimension=0,
        tiled=True,
    ).astype(jnp.float32)
    return (latents.astype(jnp.float32) + gate_mod * projected).astype(jnp.bfloat16)

MESH = pl.DeviceIdType.MESH
BF = jnp.bfloat16
F32 = jnp.float32
VMEM_LIMIT = 62 * 1024 * 1024


def entry_barrier(peers):
    barrier = pltpu.get_barrier_semaphore()
    for peer in peers:
        pl.semaphore_signal(barrier, inc=1, device_id=peer, device_id_type=MESH)
    pl.semaphore_wait(barrier, len(peers))


def block_kernel(
    lat_ref, w_ref, ow_ref, mod_ref, qg_ref, kg_ref, bias_ref,
    o_ref,
    q_out, kv_out, ow_all, mod_out,
    lat_all, w_all, mod_all, nrm, att,
    loc_sem, mod_s, mod_r, lat_s, lat_r, w_s, w_r, ow_s, ow_r, kv_s, kv_r, s_sem, r_sem, ready,
):
    s = lax.axis_index("seq")
    z = lax.axis_index("fsdp")
    me = s * 4 + z
    rows = lat_ref.shape[0]
    yp = lax.rem(s + 2, 4)
    cp = s + 1 - 2 * lax.rem(s, 2)
    far = 3 - s
    g = lax.axis_index("group")
    across = {"group": 1 - g}
    half = w_ref.shape[1] // 2
    mine = pl.ds(pl.multiple_of(g * half, half), half)
    theirs = pl.ds(pl.multiple_of((1 - g) * half, half), half)

    def flat_peer(step):
        peer = lax.rem(me + step, 16)
        return {"seq": peer // 4, "fsdp": lax.rem(peer, 4)}

    entry_barrier([flat_peer(step) for step in range(1, 16)] + [across])

    def remote(src, dst, ss, rs, dev):
        return pltpu.make_async_remote_copy(
            src_ref=src, dst_ref=dst, send_sem=ss, recv_sem=rs, device_id=dev, device_id_type=MESH
        )

    def mod_copy(step):
        return remote(
            mod_ref, mod_all.at[me], mod_s.at[step - 1], mod_r.at[step - 1], flat_peer(step)
        )

    for step in range(1, 16):
        mod_copy(step).start()

    def lat_copy(side, k):
        target = z + 1 if side == 0 else z - 1
        shard = z - k if side == 0 else z + k
        shard = jnp.clip(shard, 0, 3)
        src = lat_ref if k == 0 else lat_all.at[shard]
        return remote(
            src, lat_all.at[shard], lat_s.at[side, k], lat_r.at[side, k], {"fsdp": target}
        )

    def sends(side, k):
        return (z < 3) & (z - k >= 0) if side == 0 else (z > 0) & (z + k <= 3)

    def gets(side, k):
        return z - 1 - k >= 0 if side == 0 else z + 1 + k <= 3

    def start_lat(k):
        for side in range(2):
            @pl.when(sends(side, k))
            def _():
                lat_copy(side, k).start()

    def wait_lat(k):
        for side in range(2):
            @pl.when(gets(side, k))
            def _():
                remote(
                    lat_ref,
                    lat_all.at[jnp.clip(z - 1 - k if side == 0 else z + 1 + k, 0, 3)],
                    lat_s.at[side, k], lat_r.at[side, k], {"fsdp": lax.rem(z + 1, 4)},
                ).wait_recv()

    start_lat(0)

    def spread(own, full, sems_s, sems_r):
        def copy(kind):
            src, dst, dev = (
                (own.at[mine], full.at[s, mine], {"seq": yp}),
                (own, full.at[s], {"seq": cp}),
                (full.at[yp, mine], full.at[yp, mine], {"seq": cp}),
                (full.at[yp, mine], full.at[yp, mine], across),
                (full.at[yp, theirs], full.at[yp, theirs], {"seq": cp}),
            )[kind]
            return remote(src, dst, sems_s.at[kind], sems_r.at[kind], dev)

        def wait(kind):
            slot = (yp, cp, far, yp, far)[kind]
            part = (mine, None, mine, theirs, theirs)[kind]
            src = own if part is None else own.at[part]
            dst = full.at[slot] if part is None else full.at[slot, part]
            remote(src, dst, sems_s.at[kind], sems_r.at[kind], {"seq": cp}).wait_recv()

        return copy, wait

    w_moves = [
        spread(w_ref.at[j], w_all.at[j], w_s.at[j], w_r.at[j]) for j in range(3)
    ]
    ow_copy, ow_wait = spread(ow_ref, ow_all, ow_s, ow_r)

    def w_copy(kind, j):
        return w_moves[j][0](kind)

    def w_wait(kind, j):
        w_moves[j][1](kind)

    def after_y(copy, wait):
        wait(0)
        copy(2).start()
        copy(3).start()

    def after_x(copy, wait):
        wait(3)
        copy(4).start()

    order = (1, 2, 0)
    for j in order:
        w_copy(0, j).start()
        w_copy(1, j).start()

    local = [
        pltpu.make_async_copy(w_ref.at[0], w_all.at[0, s], loc_sem.at[0]),
        pltpu.make_async_copy(w_ref.at[1], w_all.at[1, s], loc_sem.at[4]),
        pltpu.make_async_copy(w_ref.at[2], w_all.at[2, s], loc_sem.at[5]),
        pltpu.make_async_copy(lat_ref, lat_all.at[z], loc_sem.at[1]),
        pltpu.make_async_copy(ow_ref, ow_all.at[s], loc_sem.at[2]),
        pltpu.make_async_copy(mod_ref, mod_all.at[me], loc_sem.at[3]),
    ]
    for copy in local:
        copy.start()

    @pl.when(s == 0)
    def _():
        kv_out[0] = jnp.zeros(kv_out.shape[1:], BF)

    @pl.when(s == 3)
    def _():
        kv_out[2] = jnp.zeros(kv_out.shape[1:], BF)

    for copy in local:
        copy.wait()
    for step in range(1, 16):
        sender = lax.rem(me - step + 16, 16)
        remote(
            mod_ref, mod_all.at[sender], mod_s.at[step - 1], mod_r.at[step - 1], flat_peer(step)
        ).wait_recv()
    mod_out[...] = jnp.concatenate([mod_all[i] for i in range(16)], axis=1)

    after_y(*w_moves[order[0]])
    after_y(*w_moves[order[1]])
    after_x(*w_moves[order[0]])
    wait_lat(0)
    start_lat(1)
    after_y(*w_moves[order[2]])
    ow_copy(0).start()
    ow_copy(1).start()
    after_x(*w_moves[order[1]])
    after_x(*w_moves[order[2]])
    wait_lat(1)
    start_lat(2)
    for j in order:
        for kind in (1, 2, 4):
            w_wait(kind, j)

    def kv_copy(side, i, zz):
        src = kv_out.at[1, pl.ds(pl.multiple_of(zz * rows, rows), rows)]
        dst = kv_out.at[0 if side == 0 else 2, pl.ds(pl.multiple_of(zz * rows, rows), rows)]
        target = s + 1 if side == 0 else s - 1
        return remote(src, dst, kv_s.at[side, i], kv_r.at[side, i], {"seq": target})

    hi = z // 2

    def shard_of(i):
        return i + hi * (3 - 2 * i)

    width = w_ref.shape[1]
    lane = 128

    def one_shard(i, carry):
        zz = shard_of(i)

        @pl.when(i == 1)
        def _():
            after_y(ow_copy, ow_wait)

        @pl.when(i == 2)
        def _():
            after_x(ow_copy, ow_wait)

        @pl.when(i == 3)
        def _():
            wait_lat(2)

        def norm_rows(r, c):
            at = pl.ds(pl.multiple_of(r * 32, 32), 32)
            values = lat_all[zz, at, :].astype(F32)
            centre = jnp.mean(values, axis=-1, keepdims=True)
            values = values - centre
            spread = jnp.mean(values * values, axis=-1, keepdims=True)
            normal = values * lax.rsqrt(spread + 1e-06)
            nrm[at, :] = (normal * (1.0 + mod_out[1:2, :]) + mod_out[0:1, :]).astype(BF)
            return c

        lax.fori_loop(0, rows // 32, norm_rows, 0)
        base = pl.ds(pl.multiple_of(zz * rows, rows), rows)
        for j in order:
            for col in range(0, width, 256):
                acc = jnp.zeros((rows, 256), F32)
                for t in range(4):
                    acc = acc + jnp.dot(
                        nrm[:, t * width : (t + 1) * width],
                        w_all[j, t, :, col : col + 256],
                        preferred_element_type=F32,
                    )
                for half in range(0, 256, lane):
                    part = acc[:, half : half + lane]
                    if j < 2:
                        gain = (qg_ref if j == 0 else kg_ref)[...]
                        scale = lax.rsqrt(jnp.mean(part * part, axis=-1, keepdims=True) + 1e-06)
                        part = part * scale * gain
                    part = part.astype(BF)
                    first = col + half
                    if j == 0:
                        q_out[base, first : first + lane] = part
                    else:
                        first = first + (j - 1) * width
                        kv_out[1, base, first : first + lane] = part
            if j == 2:
                @pl.when(s < 3)
                def _():
                    kv_copy(0, i, zz).start()

                @pl.when(s > 0)
                def _():
                    kv_copy(1, i, zz).start()
        return carry

    lax.fori_loop(0, 4, one_shard, 0)

    for k in range(3):
        for side in range(2):
            @pl.when(sends(side, k))
            def _():
                lat_copy(side, k).wait_send()
    for kind in range(5):
        for j in range(3):
            w_copy(kind, j).wait_send()
    for step in range(1, 4):
        pl.semaphore_signal(
            ready, inc=1, device_id={"fsdp": lax.rem(z + step, 4)}, device_id_type=MESH
        )
    for i in range(4):
        @pl.when(s > 0)
        def _():
            kv_copy(0, i, shard_of(i)).wait_recv()

        @pl.when(s < 3)
        def _():
            kv_copy(1, i, shard_of(i)).wait_recv()

    heads = width // HD
    keys = 3 * 4 * rows
    far_outer = 3 - 3 * hi
    far_inner = 2 - hi
    near = z + 1 - 2 * lax.rem(z, 2)
    inner = (z == 1) | (z == 2)

    def slab(n):
        if isinstance(n, int):
            return w_all.at[n // 3, :, n % 3 * rows : (n % 3 + 1) * rows, :]
        at = pl.ds(pl.multiple_of(lax.rem(n, 3) * rows, rows), rows)
        return w_all.at[n // 3, :, at, :]

    def send(src, dst, goal):
        return remote(slab(src), slab(4 + dst), s_sem.at[src], r_sem.at[dst], {"fsdp": goal})

    to_near = [send(src, src, near) for src in range(3)]
    to_far = [send(0, 3, far_outer), send(1, 3, far_inner)]

    def attend_rows(goal):
        base = pl.ds(pl.multiple_of(goal * rows, rows), rows)
        tiles = rows // TILE

        def head(h, c):
            at = pl.ds(pl.multiple_of(h * HD, HD), HD)
            values_at = pl.ds(pl.multiple_of((heads + h) * HD, HD), HD)
            scores = lax.dot_general(
                q_out[base, at], kv_out[:, :, at].reshape(keys, HD), (((1,), (1,)), ((), ())),
                preferred_element_type=F32,
            )
            bias = bias_ref[pl.ds(goal * tiles, tiles)]
            scores = (scores.reshape(tiles, TILE, keys) + bias).reshape(rows, keys)
            top = jnp.max(scores, axis=1, keepdims=True)
            weights = jnp.exp2((scores - top) * (math.log2(math.e) / math.sqrt(HD)))
            total = jnp.sum(weights, axis=1, keepdims=True)
            mixed = jnp.dot(
                weights.astype(BF), kv_out[:, :, values_at].reshape(keys, HD),
                preferred_element_type=F32,
            )
            att[:, at] = (mixed / total).astype(BF)
            return c

        lax.fori_loop(0, heads, head, 0)

    def add_near(slot):
        to_near[slot].wait_recv()
        dst, src = slab(slot), slab(4 + slot)

        def add(r, c):
            at = pl.ds(pl.multiple_of(r * 32, 32), 32)
            dst[:, at, :] = (dst[:, at, :].astype(F32) + src[:, at, :].astype(F32)).astype(BF)
            return c

        lax.fori_loop(0, rows // 32, add, 0)
        to_far[slot].start()

    def step(i, c):
        goal = jnp.where(i == 0, far_outer, jnp.where(i == 1, far_inner, jnp.where(i == 2, near, z)))
        attend_rows(goal)

        @pl.when(i == 0)
        def _():
            for kind in (1, 2, 4):
                ow_wait(kind)

        dst = slab(i)
        for t in range(4):
            dst[t] = jnp.dot(att[...], ow_all[t], preferred_element_type=F32).astype(BF)

        @pl.when(i == 0)
        def _():
            pl.semaphore_wait(ready, 3)

        for slot in range(2):
            @pl.when(jnp.logical_not(inner) & (i == slot))
            def _():
                to_near[slot].start()

        @pl.when(i == 2)
        def _():
            to_near[2].start()

        @pl.when(inner & (i == 2))
        def _():
            add_near(0)

        @pl.when(inner & (i == 3))
        def _():
            add_near(1)

        return c

    lax.fori_loop(0, 4, step, 0)
    to_near[2].wait_recv()
    send(0, 3, far_outer).wait_recv()
    own, direct, summed = slab(3), slab(6), slab(7)

    def finish(r, c):
        at = pl.ds(pl.multiple_of(r * 32, 32), 32)
        for t in range(4):
            cols = slice(t * width, (t + 1) * width)
            total = own[t, at, :].astype(F32)
            total = total + direct[t, at, :].astype(F32)
            total = total + summed[t, at, :].astype(F32)
            o_ref[at, cols] = (
                lat_ref[at, cols].astype(F32) + mod_out[2:3, cols] * total
            ).astype(BF)
        return c

    lax.fori_loop(0, rows // 32, finish, 0)
    for slot in range(3):
        to_near[slot].wait_send()
    for i in range(4):
        @pl.when(s < 3)
        def _():
            kv_copy(0, i, shard_of(i)).wait_send()

        @pl.when(s > 0)
        def _():
            kv_copy(1, i, shard_of(i)).wait_send()
    for step_id in range(1, 16):
        mod_copy(step_id).wait_send()
    for kind in range(5):
        ow_copy(kind).wait_send()


def whole_block(latents, w, ow, mod, q_gain, k_gain, bias):
    rows, model = latents.shape
    width = w.shape[1]
    vmem = pl.BlockSpec(memory_space=pltpu.VMEM)
    place = pl.BlockSpec(memory_space=pl.ANY)
    dma = pltpu.SemaphoreType.DMA
    return pl.pallas_call(
        block_kernel,
        out_shape=jax.ShapeDtypeStruct(latents.shape, BF),
        in_specs=[vmem, place, place, vmem, vmem, vmem, vmem],
        out_specs=vmem,
        scratch_shapes=[
            pltpu.VMEM((4 * rows, width), BF),
            pltpu.VMEM((3, 4 * rows, 2 * width), BF),
            pltpu.VMEM((4,) + ow.shape, BF),
            pltpu.VMEM((8, model), F32),
            pltpu.VMEM((4, rows, model), BF),
            pltpu.VMEM((3, 4) + w.shape[1:], BF),
            pltpu.VMEM((16,) + mod.shape, F32),
            pltpu.VMEM((rows, model), BF),
            pltpu.VMEM((rows, width), BF),
            dma((6,)), dma((15,)), dma((15,)), dma((2, 3)), dma((2, 3)),
            dma((3, 5)), dma((3, 5)), dma((5,)), dma((5,)), dma((2, 4)), dma((2, 4)),
            dma((4,)), dma((4,)), pltpu.SemaphoreType.REGULAR,
        ],
        compiler_params=pltpu.CompilerParams(
            collective_id=0, has_side_effects=True, vmem_limit_bytes=VMEM_LIMIT
        ),
    )(latents, w, ow, mod, q_gain, k_gain, bias)


def key_bias(tile_slot, win_start, block_idx):
    blocks_total, spot_count = tile_slot.shape
    ids_query = lax.dynamic_index_in_dim(tile_slot, block_idx, 0, keepdims=False)
    window_row = lax.dynamic_index_in_dim(win_start, block_idx, 0, keepdims=False)
    onehot = ids_query[:, None] == jnp.arange(spot_count, dtype=jnp.int32)[None, :]
    corner = jnp.sum(jnp.where(onehot[:, :, None], window_row[None], 0), axis=1)
    result = []
    for offset in (-1, 0, 1):
        key_time = block_idx + offset
        ids_key = lax.dynamic_index_in_dim(
            tile_slot, jnp.clip(key_time, 0, blocks_total - 1), 0, keepdims=False
        )
        row = (ids_key // GW)[None]
        col = (ids_key % GW)[None]
        inside = (corner[:, 0:1] <= key_time) & (key_time <= corner[:, 0:1] + 1)
        inside = inside & (corner[:, 1:2] <= row) & (row <= corner[:, 1:2] + 2)
        inside = inside & (corner[:, 2:3] <= col) & (col <= corner[:, 2:3] + 2)
        result.append(inside)
    inside = jnp.concatenate(result, axis=1)
    bias = jnp.where(inside, 0.0, -1e30).astype(F32)
    return jnp.repeat(bias, TILE, axis=1)[:, None, :]


def fast_body(
    latents, qkv_weight, out_weight, mod_weight, q_gain, k_gain, tile_slot, win_start, step_index
):
    signal = time_signal(step_index)
    local_cols = mod_weight.shape[2]
    own_mod = jnp.dot(
        signal[None], mod_weight.reshape(FREQ, 3 * local_cols), preferred_element_type=F32
    ).reshape(3, local_cols)
    own_mod = jnp.pad(own_mod, ((0, 5), (0, 0)))
    w = jnp.transpose(qkv_weight, (1, 0, 2))
    bias = key_bias(tile_slot, win_start, lax.axis_index("seq"))
    return whole_block(latents, w, out_weight, own_mod, q_gain[None], k_gain[None], bias)


def solution(mesh):
    in_specs = (
        P(("group", "seq", "fsdp"), None),
        P("seq", None, "fsdp"),
        P("fsdp", "seq"),
        P(None, None, ("seq", "fsdp")),
        P(),
        P(),
        P("group", None),
        P("group", None, None),
        P("group"),
    )
    out_specs = P(("group", "seq", "fsdp"), None)
    small = mesh.shape["seq"] == 4 and mesh.shape["fsdp"] == 4
    return jax.shard_map(
        fast_body if small else body,
        mesh=mesh, in_specs=in_specs, out_specs=out_specs, check_vma=False,
    )
```
